512 devices in a mesh: gz: 8 (over z), pr: 16 (over y, core), pc: 4 (over x).
Axes of the slice: x: 4, y: 8, z: 8, core: 2. Of those that a mesh axis runs over, the one named last changes fastest.
Arguments:
- sep_rhs: bfloat16 [16, 3, 128, 128], P('pr'), may hold values from -6 to 6
- diag_inverse: bfloat16 [16, 3, 128, 128], P('pr'), may hold values from -0.5 to 0.5
- off_blocks: bfloat16 [16, 3, 12, 4, 128, 128], P('pr', None, None, 'pc'), may hold values from -0.109375 to 0.109375
- pattern: int32 [48, 48], replicated, may hold values 0 or 1
- sub_solution: bfloat16 [8, 16, 4, 1024, 128], P('gz', 'pr', 'pc'), may hold values from -6 to 6
- couple_low: bfloat16 [8, 16, 4, 384, 1024], P('gz', 'pr', 'pc'), may hold values from -0.03125 to 0.03125
- couple_up: bfloat16 [8, 16, 4, 1024, 384], P('gz', 'pr', 'pc'), may hold values from -0.3125 to 0.3125
Outputs:
- sep_solution: bfloat16 [16, 3, 128, 128], P('pr')
- sub_result: bfloat16 [8, 16, 4, 1024, 128], P('gz', 'pr', 'pc')
The draws below stay inside these ranges and needn't reach their ends.
Inputs may be any that keep to these rules, and one draw needn't show every extreme that they name: `pattern`: only entries [i, j] with i // 16 > j // 16 are read; 1 marks a nonzero block.
All inputs are finite; a program needn't handle non-finite values.
Results may differ from the reference program's by a relative error of at most 0.02.
Values may be sent and summed in bfloat16 or wider, within the bound.
A program may use at most 64 MiB of HBM per device.

```python
import jax
import jax.numpy as jnp
from jax import lax

S = 128
R = 128
SUB = 1024
RB = 3
NS = 48
CB = 12
N_GZ = 8
N_PR = 16
N_PC = 4


def with_ends(values, rng, least, largest):
    longest = values.shape.index(max(values.shape))
    spots = []
    for shift in (0, 1):
        where = [jax.random.randint(jax.random.fold_in(rng, axis), (), 0, length) for axis, length in enumerate(values.shape)]
        where[longest] = (where[longest] + shift) % values.shape[longest]
        spots.append(tuple(where))
    return values.at[spots[0]].set(least).at[spots[1]].set(largest)


def block_scale(key, shape, split, least, top_value):
    factor_of, own = 1.0, jax.random.fold_in(key, 6)
    for dim, shards_of in split:
        draws = jnp.exp(jax.random.uniform(jax.random.fold_in(own, dim), (shards_of,), jnp.float32, least / len(split), top_value / len(split)))
        factor_of = factor_of * jnp.repeat(draws, shape[dim] // shards_of).reshape([-1 if axis == dim else 1 for axis in range(len(shape))])
    return factor_of


def bell_draw(rng, shape, scale, bound, pieces=(), held_as=jnp.bfloat16):
    loudness = block_scale(rng, shape, pieces, -0.22, 0.18) if pieces else 1.0
    entries = jax.random.normal(rng, shape, jnp.float32) * scale * loudness
    return jnp.minimum(jnp.maximum(entries, -bound), bound).astype(held_as)


def setup_inputs(seed: int = 0) -> dict:
    streams_of = jax.random.split(jax.random.key(seed), 8)
    sep_rhs = bell_draw(streams_of[0], (N_PR, RB, S, R), 1.0, 6.0, ((0, 16),))
    diag_inverse = bell_draw(streams_of[1], (N_PR, RB, S, S), S ** -0.5, 0.5, ((0, 16),))
    off_blocks = bell_draw(streams_of[2], (N_PR, RB, CB, N_PC, S, S), (S * NS // 2) ** -0.5, 0.109375, ((0, 16), (3, 4)))
    pattern = with_ends((jax.random.randint(streams_of[3], (NS, NS), 0, 2) < 1).astype(jnp.int32), jax.random.fold_in(streams_of[3], 1), 0, 1)
    sub_solution = bell_draw(streams_of[4], (N_GZ, N_PR, N_PC, SUB, R), 1.0, 6.0, ((0, 8), (1, 16), (2, 4)))
    couple_low = bell_draw(streams_of[5], (N_GZ, N_PR, N_PC, RB * S, SUB), (SUB * N_GZ * N_PC) ** -0.5, 0.03125, ((0, 8), (1, 16), (2, 4)))
    couple_up = bell_draw(streams_of[6], (N_GZ, N_PR, N_PC, SUB, RB * S), (RB * S) ** -0.5, 0.3125, ((0, 8), (1, 16), (2, 4)))
    return {"sep_rhs": sep_rhs, "diag_inverse": diag_inverse, "off_blocks": off_blocks, "pattern": pattern, "sub_solution": sub_solution, "couple_low": couple_low, "couple_up": couple_up}


def couple_term(pair_args):
    return jnp.dot(pair_args[0], pair_args[1], preferred_element_type=jnp.float32)


def reference(sep_rhs, diag_inverse, off_blocks, pattern, sub_solution, couple_low, couple_up):
    count_all = N_GZ * N_PR * N_PC
    low_flat = couple_low.reshape(count_all, RB * S, SUB)
    sub_flat = sub_solution.reshape(count_all, SUB, R)
    terms = lax.map(couple_term, (low_flat, sub_flat))
    terms = terms.reshape(N_GZ, N_PR, N_PC, RB, S, R)
    summed = jnp.sum(jnp.sum(terms, axis=2), axis=0)
    fed_rhs = sep_rhs.astype(jnp.float32) - summed
    y_list = []
    for i in range(NS):
        prow, arow = i % N_PR, i // N_PR
        parts = [jnp.zeros((S, R), jnp.float32) for q in range(N_PC)]
        for j in range(NS):
            if j // N_PR < arow:
                product = jnp.dot(off_blocks[prow, arow, j // N_PC, j % N_PC], y_list[j], preferred_element_type=jnp.float32)
                parts[j % N_PC] = parts[j % N_PC] + jnp.where(pattern[i, j] == 1, product, 0.0)
        lowsum = jnp.zeros((S, R), jnp.float32)
        for q in range(N_PC):
            lowsum = lowsum + parts[q].astype(jnp.bfloat16).astype(jnp.float32)
        resid = (fed_rhs[prow, arow] - lowsum).astype(jnp.bfloat16)
        y_list.append(jnp.dot(diag_inverse[prow, arow], resid, preferred_element_type=jnp.float32).astype(jnp.bfloat16))
    x_list = [None] * NS
    for i in range(NS - 1, -1, -1):
        prow, arow = i % N_PR, i // N_PR
        parts = [jnp.zeros((S, R), jnp.float32) for q in range(N_PC)]
        for j in range(NS):
            if j // N_PR > arow:
                product = jnp.dot(off_blocks[prow, arow, j // N_PC, j % N_PC], x_list[j], preferred_element_type=jnp.float32)
                parts[j % N_PC] = parts[j % N_PC] + jnp.where(pattern[j, i] == 1, product, 0.0)
        upsum = jnp.zeros((S, R), jnp.float32)
        for q in range(N_PC):
            upsum = upsum + parts[q].astype(jnp.bfloat16).astype(jnp.float32)
        x_list[i] = (y_list[i].astype(jnp.float32) - upsum).astype(jnp.bfloat16)
    stacked = jnp.stack(x_list).reshape(RB, N_PR, S, R)
    sep_solution = jnp.transpose(stacked, (1, 0, 2, 3))
    x_rows = sep_solution.reshape(N_PR, RB * S, R)
    up_flat = couple_up.reshape(count_all, SUB, RB * S)
    owners = (jnp.arange(count_all, dtype=jnp.int32) // N_PC) % N_PR

    def remove_term(pair_args):
        own_rows = lax.dynamic_index_in_dim(x_rows, pair_args[2], 0, keepdims=False)
        product = jnp.dot(pair_args[0], own_rows, preferred_element_type=jnp.float32)
        return (pair_args[1].astype(jnp.float32) - product).astype(jnp.bfloat16)

    sub_result = lax.map(remove_term, (up_flat, sub_flat, owners))
    return sep_solution, sub_result.reshape(N_GZ, N_PR, N_PC, SUB, R)
```

```python
import functools

import jax
import jax.numpy as jnp
from jax import lax
from jax.experimental import pallas as pl
from jax.experimental.pallas import tpu as pltpu
from jax.sharding import PartitionSpec as P

F32 = jnp.float32
BF16 = jnp.bfloat16
MESH = pl.DeviceIdType.MESH


def nt(a, b):
    return lax.dot_general(a, b, (((1,), (1,)), ((), ())), preferred_element_type=F32)


def ring_order(n):
    return sorted(range(1, n), key=lambda r: (-min(r, n - r), r))


def kernel(
    dims,
    rhs_hbm, inv_hbm, blk_hbm, pat_hbm, sub_hbm, low_hbm, up_hbm,
    x_hbm, res_hbm,
    sub_v, low_v, up_v, inv_v, rhs_v, blk_v, pat_s,
    w_v, rhs_t, zsend, zrecv, fsend, frecv, psend, precv, ysend, yrecv, xz, acc, res_v, x_v,
    in_sem, zs_sem, zr_sem, fs_sem, fr_sem, ps_sem, pr_sem, ys_sem, yr_sem, xs_sem, xr_sem, out_sem,
):
    n_g, n_p, n_q, levels, width, n_b = dims
    g = lax.axis_index("gz")
    p = lax.axis_index("pr")
    q = lax.axis_index("pc")
    nb = n_p // n_q
    own = lax.rem(p, n_q) == q
    own_b = p // n_q

    loads = [
        pltpu.make_async_copy(sub_hbm, sub_v, in_sem.at[0]),
        pltpu.make_async_copy(low_hbm.at[pl.ds(0, width)], low_v.at[pl.ds(0, width)], in_sem.at[1]),
        pltpu.make_async_copy(
            low_hbm.at[pl.ds(width, (levels - 1) * width)],
            low_v.at[pl.ds(width, (levels - 1) * width)],
            in_sem.at[2],
        ),
        pltpu.make_async_copy(rhs_hbm, rhs_v, in_sem.at[3]),
        pltpu.make_async_copy(inv_hbm, inv_v, in_sem.at[4]),
        pltpu.make_async_copy(pat_hbm, pat_s, in_sem.at[5]),
        pltpu.make_async_copy(blk_hbm, blk_v, in_sem.at[6]),
        pltpu.make_async_copy(up_hbm, up_v, in_sem.at[7]),
    ]
    for c in loads:
        c.start()

    def z_peer(r):
        return {"gz": lax.rem(g + r, n_g)}

    def x_peer(r):
        return {"pc": lax.rem(q + r, n_q)}

    def y_peer(r):
        return {"pr": lax.rem(p + r, n_p)}

    barrier = pltpu.get_barrier_semaphore()
    for r in ring_order(n_g):
        pl.semaphore_signal(barrier, inc=1, device_id=z_peer(r), device_id_type=MESH)
    for r in ring_order(n_p):
        pl.semaphore_signal(barrier, inc=1, device_id=y_peer(r), device_id_type=MESH)
    for r in ring_order(n_q):
        pl.semaphore_signal(barrier, inc=1, device_id=x_peer(r), device_id_type=MESH)

    def remote(src, dst, ssem, rsem, peer):
        return pltpu.make_async_remote_copy(
            src_ref=src, dst_ref=dst, send_sem=ssem, recv_sem=rsem, device_id=peer, device_id_type=MESH
        )

    sends = []

    def partial_update(a):
        part = jnp.dot(low_v[a * width : (a + 1) * width, :], sub_v[...], preferred_element_type=F32)
        flipped = jnp.transpose(part).astype(BF16)
        zsend[a] = flipped.reshape(n_g, flipped.shape[0] // n_g, width)

    def z_copy(a, r):
        return remote(
            zsend.at[a, lax.rem(g + r, n_g)], zrecv.at[a, r - 1], zs_sem.at[a, r - 1], zr_sem.at[a, r - 1], z_peer(r)
        )

    loads[0].wait()
    loads[1].wait()
    partial_update(0)
    pl.semaphore_wait(barrier, n_g + n_p + n_q - 3)
    for r in ring_order(n_g):
        c = z_copy(0, r)
        c.start()
        sends.append(c)
    loads[2].wait()
    for a in range(1, levels):
        partial_update(a)
        for r in ring_order(n_g):
            c = z_copy(a, r)
            c.start()
            sends.append(c)

    loads[3].wait()
    for a in range(levels):
        rhs_t[a] = jnp.transpose(rhs_v[a].astype(F32)).reshape(n_g, rhs_t.shape[2], width)
    loads[4].wait()
    loads[5].wait()
    loads[6].wait()

    def masked_blocks(row_level, col_level):
        slot = row_level * (levels - 1) + (col_level if col_level < row_level else col_level - 1)
        for b in range(nb):
            i = row_level * n_p + p
            j = col_level * n_p + b * n_q + q
            mark = pat_s[i, j] if col_level < row_level else pat_s[j, i]
            block = blk_v[row_level, col_level * nb + b]
            w_v[slot, :, b * width : (b + 1) * width] = jnp.where(mark == 1, block, jnp.zeros_like(block))

    def weights(row_level, col_level):
        slot = row_level * (levels - 1) + (col_level if col_level < row_level else col_level - 1)
        return w_v[slot]

    for col in range(levels):
        for row in range(col + 1, levels):
            masked_blocks(row, col)

    def z_total(a):
        for r in range(1, n_g):
            z_copy(a, r).wait_recv()
        total = zsend[a, g].astype(F32)
        for r in range(1, n_g):
            total = total + zrecv[a, r - 1].astype(F32)
        return total.astype(BF16)

    def exchange(value, src, dst, ssem, rsem):
        src[...] = value
        copies = []
        for r in ring_order(n_q):
            c = remote(src, dst.at[r - 1], ssem.at[r - 1], rsem.at[r - 1], x_peer(r))
            c.start()
            copies.append(c)
            sends.append(c)
        return copies

    def collected(value, copies, dst):
        for c in copies:
            c.wait_recv()
        half = n_q // 2
        total = None
        for k in range(half):
            first = value.astype(F32) if k == 0 else dst[k - 1].astype(F32)
            pair = first + dst[k + half - 1].astype(F32)
            total = pair if total is None else total + pair
        return total

    def f_exchange(a):
        value = z_total(a)
        return value, exchange(value, fsend.at[a], frecv.at[a], fs_sem.at[a], fr_sem.at[a])

    def fed(a, started):
        value, copies = started
        return rhs_t[a, g] - collected(value, copies, frecv.at[a])

    def y_copy(k, r):
        return remote(ysend.at[k], yrecv.at[k, own_b], ys_sem.at[k, r - 1], yr_sem.at[k, own_b], y_peer(r))

    def broadcast(k, value):
        ysend[k] = value

        @pl.when(own)
        def _():
            for r in ring_order(n_p):
                y_copy(k, r).start()
            yrecv[k, own_b] = value

    def gathered(k):
        for b in range(nb):

            @pl.when(b * n_q + q != p)
            def _(b=b):
                remote(ysend.at[k], yrecv.at[k, b], ys_sem.at[k, 0], yr_sem.at[k, b], y_peer(1)).wait_recv()

        return jnp.concatenate([yrecv[k, b] for b in range(nb)], axis=1)

    def spread(a, value):
        xz[a, g] = value
        for r in ring_order(n_g):
            c = remote(xz.at[a, g], xz.at[a, g], xs_sem.at[a, r - 1], xr_sem.at[a, r - 1], z_peer(r))
            c.start()
            sends.append(c)

    def solve(a, resid):
        return nt(resid.astype(BF16), inv_v[a]).astype(BF16)

    started = f_exchange(0)
    fed_a = fed(0, started)
    y = [solve(0, fed_a)]
    broadcast(0, y[0])
    later = [f_exchange(a) for a in range(1, levels)]
    for row in range(levels):
        for col in range(row + 1, levels):
            masked_blocks(row, col)
    feds = [None] + [fed(a, later[a - 1]) for a in range(1, levels)]

    pending = [None] * levels
    for a in range(1, levels):
        block = gathered(a - 1)
        part = nt(block, weights(a, a - 1))
        part = part if pending[a] is None else pending[a] + part
        value = part.astype(BF16)
        copies = exchange(value, psend.at[a - 1], precv.at[a - 1], ps_sem.at[a - 1], pr_sem.at[a - 1])
        for later_a in range(a + 1, levels):
            more = nt(block, weights(later_a, a - 1))
            pending[later_a] = more if pending[later_a] is None else pending[later_a] + more
        total = collected(value, copies, precv.at[a - 1])
        y.append(solve(a, feds[a] - total))
        broadcast(a, y[a])

    spread(levels - 1, y[levels - 1])
    pending = [None] * levels
    for a in range(levels - 2, -1, -1):
        k = 2 * (levels - 1) - 1 - a
        source = {levels - 2: levels - 1}.get(a, levels + (levels - 2 - (a + 1)))
        block = gathered(source)
        part = nt(block, weights(a, a + 1))
        part = part if pending[a] is None else pending[a] + part
        value = part.astype(BF16)
        copies = exchange(value, psend.at[k], precv.at[k], ps_sem.at[k], pr_sem.at[k])
        for later_a in range(a - 1, -1, -1):
            more = nt(block, weights(later_a, a + 1))
            pending[later_a] = more if pending[later_a] is None else pending[later_a] + more
        total = collected(value, copies, precv.at[k])
        x = (y[a].astype(F32) - total).astype(BF16)
        if a > 0:
            broadcast(levels + (levels - 2 - a), x)
        spread(a, x)

    loads[7].wait()
    rows = res_v.shape[0]
    n_c = 4
    chunk = rows // n_c
    stores = []
    for a in range(levels - 1, -1, -1):
        for r in range(1, n_g):
            remote(xz.at[a, g], xz.at[a, g], xs_sem.at[a, r - 1], xr_sem.at[a, r - 1], z_peer(r)).wait_recv()
        full = xz[a].reshape(n_g * xz.shape[2], width)
        for c in range(n_c):
            span = pl.ds(c * chunk, chunk)
            before = sub_v[span, :].astype(F32) if a == levels - 1 else acc[span, :]
            after = before - nt(up_v[span, a * width : (a + 1) * width], full)
            if a > 0:
                acc[span, :] = after
            else:
                res_v[span, :] = after.astype(BF16)
                store = pltpu.make_async_copy(res_v.at[span], res_hbm.at[span], out_sem.at[c])
                store.start()
                stores.append(store)
        x_v[a] = jnp.transpose(full.astype(F32)).astype(BF16)
    store = pltpu.make_async_copy(x_v, x_hbm, out_sem.at[n_c])
    store.start()
    stores.append(store)

    for c in sends:
        c.wait_send()

    @pl.when(own)
    def _():
        for k in range(2 * levels - 2):
            for r in range(1, n_p):
                y_copy(k, r).wait_send()

    for store in stores:
        store.wait()


def per_device(dims, sep_rhs, diag_inverse, off_blocks, pattern, sub_solution, couple_low, couple_up):
    n_g, n_p, n_q, levels, width, n_b = dims
    sub = sub_solution.reshape(sub_solution.shape[-2:])
    low = couple_low.reshape(couple_low.shape[-2:])
    up = couple_up.reshape(couple_up.shape[-2:])
    rhs = sep_rhs.reshape(sep_rhs.shape[1:])
    inv = diag_inverse.reshape(diag_inverse.shape[1:])
    blk = off_blocks.reshape(levels, n_b, width, width)
    rows, cols = sub.shape
    piece = cols // n_g
    nb = n_p // n_q
    n_bc = 2 * levels - 2
    dma = pltpu.SemaphoreType.DMA
    x, res = pl.pallas_call(
        functools.partial(kernel, dims),
        out_shape=(
            jax.ShapeDtypeStruct(rhs.shape, BF16),
            jax.ShapeDtypeStruct(sub.shape, BF16),
        ),
        in_specs=[pl.BlockSpec(memory_space=pl.ANY)] * 7,
        out_specs=(pl.BlockSpec(memory_space=pl.ANY),) * 2,
        scratch_shapes=[
            pltpu.VMEM(sub.shape, BF16),
            pltpu.VMEM(low.shape, BF16),
            pltpu.VMEM(up.shape, BF16),
            pltpu.VMEM(inv.shape, BF16),
            pltpu.VMEM(rhs.shape, BF16),
            pltpu.VMEM(blk.shape, BF16),
            pltpu.SMEM(pattern.shape, jnp.int32),
            pltpu.VMEM((levels * (levels - 1), width, nb * width), BF16),
            pltpu.VMEM((levels, n_g, piece, width), F32),
            pltpu.VMEM((levels, n_g, piece, width), BF16),
            pltpu.VMEM((levels, n_g - 1, piece, width), BF16),
            pltpu.VMEM((levels, piece, width), BF16),
            pltpu.VMEM((levels, n_q - 1, piece, width), BF16),
            pltpu.VMEM((n_bc, piece, width), BF16),
            pltpu.VMEM((n_bc, n_q - 1, piece, width), BF16),
            pltpu.VMEM((n_bc, piece, width), BF16),
            pltpu.VMEM((n_bc, nb, piece, width), BF16),
            pltpu.VMEM((levels, n_g, piece, width), BF16),
            pltpu.VMEM(sub.shape, F32),
            pltpu.VMEM(sub.shape, BF16),
            pltpu.VMEM(rhs.shape, BF16),
            dma((8,)),
            dma((levels, n_g - 1)),
            dma((levels, n_g - 1)),
            dma((levels, n_q - 1)),
            dma((levels, n_q - 1)),
            dma((n_bc, n_q - 1)),
            dma((n_bc, n_q - 1)),
            dma((n_bc, n_p - 1)),
            dma((n_bc, nb)),
            dma((levels, n_g - 1)),
            dma((levels, n_g - 1)),
            dma((5,)),
        ],
        compiler_params=pltpu.CompilerParams(collective_id=0, has_side_effects=True),
    )(rhs, inv, blk, pattern, sub, low, up)
    return x[None], res[None, None, None]


def solution(mesh):
    n_g, n_p, n_q = mesh.shape["gz"], mesh.shape["pr"], mesh.shape["pc"]

    def step(*args):
        levels, width = args[1].shape[1], args[1].shape[2]
        dims = (n_g, n_p, n_q, levels, width, args[2].shape[2])
        return per_device(dims, *args)

    return jax.shard_map(
        step,
        mesh=mesh,
        in_specs=(
            P("pr", None, None, None),
            P("pr", None, None, None),
            P("pr", None, None, "pc", None, None),
            P(),
            P("gz", "pr", "pc", None, None),
            P("gz", "pr", "pc", None, None),
            P("gz", "pr", "pc", None, None),
        ),
        out_specs=(P("pr", None, None, None), P("gz", "pr", "pc", None, None)),
        check_vma=False,
    )
```

```python
import functools

import jax
import jax.numpy as jnp
from jax import lax
from jax.experimental import pallas as pl
from jax.experimental.pallas import tpu as pltpu
from jax.sharding import PartitionSpec as P

F32 = jnp.float32
BF16 = jnp.bfloat16
MESH = pl.DeviceIdType.MESH


def nt(a, b):
    return lax.dot_general(a, b, (((1,), (1,)), ((), ())), preferred_element_type=F32)


def ring_order(n):
    return sorted(range(1, n), key=lambda r: (-min(r, n - r), r))


def kernel(
    dims,
    rhs_hbm, inv_hbm, blk_hbm, pat_hbm, sub_hbm, low_hbm, up_hbm,
    x_v, res_v,
    sub_v, low_v, up_v, inv_v, rhs_v, blk_v, pat_s,
    w_v, rhs_t, zsend, zrecv, fsend, frecv, psend, precv, bsend, brecv, ysend, yrecv, xz, acc, u_piece, u_all, f_all, prod,
    in_sem, zs_sem, zr_sem, fs_sem, fr_sem, ps_sem, pr_sem, ys_sem, yr_sem, xs_sem, xr_sem, us_sem, ur_sem, ws_sem, wr_sem, ds_sem, dr_sem,
):
    n_g, n_p, n_q, levels, width, n_b = dims
    g = lax.axis_index("gz")
    p = lax.axis_index("pr")
    q = lax.axis_index("pc")
    nb = n_p // n_q
    own = lax.rem(p, n_q) == q
    own_b = p // n_q

    part_rows = prod.shape[1]
    halves = width // part_rows

    rest = pl.ds(width, (levels - 1) * width)
    pairs = (
        (sub_hbm, sub_v),
        (low_hbm.at[pl.ds(0, width)], low_v.at[pl.ds(0, width)]),
        (low_hbm.at[rest], low_v.at[rest]),
        (blk_hbm, blk_v),
        (pat_hbm, pat_s),
        (rhs_hbm, rhs_v),
        (inv_hbm, inv_v),
        (up_hbm, up_v),
    )
    loads = [pltpu.make_async_copy(a, b, in_sem.at[k]) for k, (a, b) in enumerate(pairs)]
    for c in loads:
        c.start()

    def z_peer(r):
        return {"gz": lax.rem(g + r, n_g)}

    def x_peer(r):
        return {"pc": lax.rem(q + r, n_q)}

    def y_peer(r):
        return {"pr": lax.rem(p + r, n_p)}

    barrier = pltpu.get_barrier_semaphore()
    for r in ring_order(n_g):
        pl.semaphore_signal(barrier, inc=1, device_id=z_peer(r), device_id_type=MESH)
    for r in ring_order(n_p):
        pl.semaphore_signal(barrier, inc=1, device_id=y_peer(r), device_id_type=MESH)
    for r in ring_order(n_q):
        pl.semaphore_signal(barrier, inc=1, device_id=x_peer(r), device_id_type=MESH)

    def remote(src, dst, ssem, rsem, peer):
        return pltpu.make_async_remote_copy(
            src_ref=src, dst_ref=dst, send_sem=ssem, recv_sem=rsem, device_id=peer, device_id_type=MESH
        )

    sends = []

    def partial_update(a):
        part = jnp.dot(low_v[a * width : (a + 1) * width, :], sub_v[...], preferred_element_type=F32)
        flipped = jnp.transpose(part).astype(BF16)
        zsend[a] = flipped.reshape(n_g, flipped.shape[0] // n_g, width)

    def z_copy(a, r):
        return remote(
            zsend.at[a, lax.rem(g + r, n_g)], zrecv.at[a, r - 1], zs_sem.at[a, r - 1], zr_sem.at[a, r - 1], z_peer(r)
        )

    loads[0].wait()
    loads[1].wait()
    partial_update(0)
    pl.semaphore_wait(barrier, n_g + n_p + n_q - 3)
    for r in ring_order(n_g):
        c = z_copy(0, r)
        c.start()
        sends.append(c)
    loads[2].wait()
    for a in range(1, levels):
        partial_update(a)
        for r in ring_order(n_g):
            c = z_copy(a, r)
            c.start()
            sends.append(c)

    def slot_of(row_level, col_level):
        return row_level * (levels - 1) + (col_level if col_level < row_level else col_level - 1)

    def masked_blocks(row_level, col_level):
        for b in range(nb):
            i = row_level * n_p + p
            j = col_level * n_p + b * n_q + q
            mark = pat_s[i, j] if col_level < row_level else pat_s[j, i]
            block = blk_v[row_level, col_level * nb + b]
            w_v[slot_of(row_level, col_level), :, b * width : (b + 1) * width] = jnp.where(
                mark == 1, block, jnp.zeros_like(block)
            )

    def weights(row_level, col_level):
        return w_v[slot_of(row_level, col_level)]

    first, second = slot_of(0, 1), slot_of(1, 2)
    loads[3].wait()
    loads[4].wait()
    masked_blocks(0, 1)
    masked_blocks(1, 2)

    def f_copy(r):
        return remote(w_v.at[first], f_all.at[r - 1], ws_sem.at[r - 1], wr_sem.at[r - 1], x_peer(r))

    def u_copy(r):
        return remote(u_piece.at[g % halves], u_all.at[p], us_sem.at[r - 1], ur_sem.at[r - 1], y_peer(r))

    def d_copy(r):
        return remote(prod.at[g], prod.at[g], ds_sem.at[r - 1], dr_sem.at[r - 1], z_peer(r))

    for r in ring_order(n_q):
        c = f_copy(r)
        c.start()
        sends.append(c)
    mine = w_v[second, :, pl.ds(pl.multiple_of(g // halves * width, width), width)]
    u_piece[...] = jnp.transpose(mine.astype(F32)).astype(BF16).reshape(halves, part_rows, width)
    for r in ring_order(n_p):
        c = u_copy(r)
        c.start()
        sends.append(c)
    u_all[p] = u_piece[g % halves]

    loads[5].wait()
    for a in range(levels):
        rhs_t[a] = jnp.transpose(rhs_v[a].astype(F32)).reshape(n_g, rhs_t.shape[2], width)
    for row_level in range(1, levels):
        for col_level in range(row_level):
            masked_blocks(row_level, col_level)
    masked_blocks(0, 2)
    loads[6].wait()

    def form_product():
        for r in range(1, n_p):
            u_copy(r).wait_recv()
        total = None
        for r in range(n_q):
            if r:
                f_copy(r).wait_recv()
            left = weights(0, 1) if r == 0 else f_all[r - 1]
            from_q = lax.rem(q + n_q - r, n_q)
            right = jnp.concatenate([u_all[b * n_q + from_q] for b in range(nb)], axis=1)
            term = nt(right, left)
            total = term if total is None else total + term
        prod[g] = total.astype(BF16)
        for r in ring_order(n_g):
            c = d_copy(r)
            c.start()
            sends.append(c)

    def product():
        for r in range(1, n_g):
            d_copy(r).wait_recv()
        return prod[...].reshape(n_g * part_rows, width)

    def z_total(a):
        for r in range(1, n_g):
            z_copy(a, r).wait_recv()
        total = zsend[a, g].astype(F32)
        for r in range(1, n_g):
            total = total + zrecv[a, r - 1].astype(F32)
        return total.astype(BF16)

    def exchange(value, src, dst, ssem, rsem):
        src[...] = value
        copies = []
        for r in ring_order(n_q):
            c = remote(src, dst.at[r - 1], ssem.at[r - 1], rsem.at[r - 1], x_peer(r))
            c.start()
            copies.append(c)
            sends.append(c)
        return copies

    def collected(value, copies, dst):
        for c in copies:
            c.wait_recv()
        half = n_q // 2
        total = None
        for k in range(half):
            first = value.astype(F32) if k == 0 else dst[k - 1].astype(F32)
            pair = first + dst[k + half - 1].astype(F32)
            total = pair if total is None else total + pair
        return total

    def f_exchange(a):
        value = z_total(a)
        return value, exchange(value, fsend.at[a], frecv.at[a], fs_sem.at[a], fr_sem.at[a])

    def fed(a, started):
        value, copies = started
        return rhs_t[a, g] - collected(value, copies, frecv.at[a])

    def y_copy(k, r):
        return remote(ysend.at[k], yrecv.at[k, own_b], ys_sem.at[k, r - 1], yr_sem.at[k, own_b], y_peer(r))

    def broadcast(k, value):
        ysend[k] = value

        @pl.when(own)
        def _():
            for r in ring_order(n_p):
                y_copy(k, r).start()
            yrecv[k, own_b] = value

    def gathered(k):
        for b in range(nb):

            @pl.when(b * n_q + q != p)
            def _(b=b):
                remote(ysend.at[k], yrecv.at[k, b], ys_sem.at[k, 0], yr_sem.at[k, b], y_peer(1)).wait_recv()

        return jnp.concatenate([yrecv[k, b] for b in range(nb)], axis=1)

    def spread_copy(lo, n, r):
        mine = xz.at[g, pl.ds(lo, n)]
        return remote(mine, mine, xs_sem.at[lo, r - 1], xr_sem.at[lo, r - 1], z_peer(r))

    def spread(lo, values):
        for k, value in enumerate(values):
            xz[g, lo + k] = value
        for r in ring_order(n_g):
            c = spread_copy(lo, len(values), r)
            c.start()
            sends.append(c)

    def solve(a, resid):
        return nt(resid.astype(BF16), inv_v[a]).astype(BF16)

    started = f_exchange(0)
    y0 = solve(0, fed(0, started))
    broadcast(0, y0)
    later = [f_exchange(a) for a in (1, 2)]
    fed1, fed2 = [fed(a, later[a - 1]) for a in (1, 2)]

    block0 = gathered(0)
    value = nt(block0, weights(1, 0)).astype(BF16)
    copies = exchange(value, psend.at[0], precv.at[0], ps_sem.at[0], pr_sem.at[0])
    part2 = nt(block0, weights(2, 0))
    y1 = solve(1, fed1 - collected(value, copies, precv.at[0]))
    broadcast(1, y1)
    form_product()
    block1 = gathered(1)
    value = (part2 + nt(block1, weights(2, 1))).astype(BF16)
    copies = exchange(value, psend.at[1], precv.at[1], ps_sem.at[1], pr_sem.at[1])
    part0 = nt(block1, weights(0, 1))
    y2 = solve(2, fed2 - collected(value, copies, precv.at[1]))
    broadcast(2, y2)
    spread(2, [y2])

    weights0 = product()
    block2 = gathered(2)
    part1 = nt(block2, weights(1, 2))
    part0 = part0 + nt(block2, weights(0, 2)) - jnp.dot(block2, weights0, preferred_element_type=F32)
    both = jnp.concatenate([part0, part1], axis=1).astype(BF16)
    copies = exchange(both, bsend, brecv, ps_sem.at[2], pr_sem.at[2])

    def finish(a, full):
        for c in range(n_c):
            span = pl.ds(c * chunk, chunk)
            before = sub_v[span, :].astype(F32) if a == levels - 1 else acc[span, :]
            after = before - nt(up_v[span, a * width : (a + 1) * width], full)
            if a > 0:
                acc[span, :] = after
            else:
                res_v[span, :] = after.astype(BF16)
        x_v[a] = jnp.transpose(full.astype(F32)).astype(BF16)

    total = collected(both, copies, brecv)
    x0 = (y0.astype(F32) - total[:, :width]).astype(BF16)
    x1 = (y1.astype(F32) - total[:, width:]).astype(BF16)
    spread(0, [x0, x1])

    loads[7].wait()
    rows = res_v.shape[0]
    n_c = 4
    chunk = rows // n_c
    for lo, n in ((2, 1), (0, 2)):
        for r in range(1, n_g):
            spread_copy(lo, n, r).wait_recv()
        for a in range(lo + n - 1, lo - 1, -1):
            finish(a, xz[:, a].reshape(n_g * xz.shape[2], width))

    for c in sends:
        c.wait_send()

    @pl.when(own)
    def _():
        for k in range(levels):
            for r in range(1, n_p):
                y_copy(k, r).wait_send()


def store_kernel(x_v, res_v, x_hbm, res_hbm, sem):
    copies = [pltpu.make_async_copy(res_v, res_hbm, sem.at[0]), pltpu.make_async_copy(x_v, x_hbm, sem.at[1])]
    for c in copies:
        c.start()
    for c in copies:
        c.wait()


def per_device(dims, sep_rhs, diag_inverse, off_blocks, pattern, sub_solution, couple_low, couple_up):
    n_g, n_p, n_q, levels, width, n_b = dims
    sub = sub_solution.reshape(sub_solution.shape[-2:])
    low = couple_low.reshape(couple_low.shape[-2:])
    up = couple_up.reshape(couple_up.shape[-2:])
    rhs = sep_rhs.reshape(sep_rhs.shape[1:])
    inv = diag_inverse.reshape(diag_inverse.shape[1:])
    blk = off_blocks.reshape(levels, n_b, width, width)
    rows, cols = sub.shape
    piece = cols // n_g
    nb = n_p // n_q
    dma = pltpu.SemaphoreType.DMA
    wc = nb * width // n_g
    vmem = pltpu.VMEM
    x, res = pl.pallas_call(
        functools.partial(kernel, dims),
        out_shape=(vmem(rhs.shape, BF16), vmem(sub.shape, BF16)),
        in_specs=[pl.BlockSpec(memory_space=pl.ANY)] * 7,
        out_specs=(pl.BlockSpec(memory_space=vmem),) * 2,
        scratch_shapes=[
            vmem(sub.shape, BF16),
            vmem(low.shape, BF16),
            vmem(up.shape, BF16),
            vmem(inv.shape, BF16),
            vmem(rhs.shape, BF16),
            vmem(blk.shape, BF16),
            pltpu.SMEM(pattern.shape, jnp.int32),
            vmem((levels * (levels - 1), width, nb * width), BF16),
            vmem((levels, n_g, piece, width), F32),
            vmem((levels, n_g, piece, width), BF16),
            vmem((levels, n_g - 1, piece, width), BF16),
            vmem((levels, piece, width), BF16),
            vmem((levels, n_q - 1, piece, width), BF16),
            vmem((2, piece, width), BF16),
            vmem((2, n_q - 1, piece, width), BF16),
            vmem((piece, 2 * width), BF16),
            vmem((n_q - 1, piece, 2 * width), BF16),
            vmem((levels, piece, width), BF16),
            vmem((levels, nb, piece, width), BF16),
            vmem((n_g, levels, piece, width), BF16),
            vmem(sub.shape, F32),
            vmem((width // wc, wc, width), BF16),
            vmem((n_p, wc, width), BF16),
            vmem((n_q - 1, width, nb * width), BF16),
            vmem((n_g, wc, width), BF16),
            dma((8,)),
            dma((levels, n_g - 1)),
            dma((levels, n_g - 1)),
            dma((levels, n_q - 1)),
            dma((levels, n_q - 1)),
            dma((levels, n_q - 1)),
            dma((levels, n_q - 1)),
            dma((levels, n_p - 1)),
            dma((levels, nb)),
            dma((levels, n_g - 1)),
            dma((levels, n_g - 1)),
            dma((n_p - 1,)),
            dma((n_p - 1,)),
            dma((n_q - 1,)),
            dma((n_q - 1,)),
            dma((n_g - 1,)),
            dma((n_g - 1,)),
        ],
        compiler_params=pltpu.CompilerParams(collective_id=0, has_side_effects=True),
    )(rhs, inv, blk, pattern, sub, low, up)
    x, res = pl.pallas_call(
        store_kernel,
        out_shape=(jax.ShapeDtypeStruct(rhs.shape, BF16), jax.ShapeDtypeStruct(sub.shape, BF16)),
        in_specs=[pl.BlockSpec(memory_space=vmem)] * 2,
        out_specs=(pl.BlockSpec(memory_space=pl.ANY),) * 2,
        scratch_shapes=[dma((2,))],
    )(*(pltpu.with_memory_space_constraint(v, vmem) for v in (x, res)))
    return x[None], res[None, None, None]


def solution(mesh):
    n_g, n_p, n_q = mesh.shape["gz"], mesh.shape["pr"], mesh.shape["pc"]

    def step(*args):
        levels, width = args[1].shape[1], args[1].shape[2]
        dims = (n_g, n_p, n_q, levels, width, args[2].shape[2])
        return per_device(dims, *args)

    return jax.shard_map(
        step,
        mesh=mesh,
        in_specs=(
            P("pr", None, None, None),
            P("pr", None, None, None),
            P("pr", None, None, "pc", None, None),
            P(),
            P("gz", "pr", "pc", None, None),
            P("gz", "pr", "pc", None, None),
            P("gz", "pr", "pc", None, None),
        ),
        out_specs=(P("pr", None, None, None), P("gz", "pr", "pc", None, None)),
        check_vma=False,
    )
```

```python
import functools

import jax
import jax.numpy as jnp
from jax import lax
from jax.experimental import pallas as pl
from jax.experimental.pallas import tpu as pltpu
from jax.sharding import PartitionSpec as P

F32 = jnp.float32
BF16 = jnp.bfloat16
MESH = pl.DeviceIdType.MESH


def nt(a, b):
    return lax.dot_general(a, b, (((1,), (1,)), ((), ())), preferred_element_type=F32)


def ring_order(n):
    return sorted(range(1, n), key=lambda r: (-min(r, n - r), r))


def kernel(
    dims,
    rhs_hbm, inv_hbm, blk_hbm, pat_hbm, sub_hbm, low_hbm, up_hbm,
    x_v, res_v,
    sub_v, low_v, up_v, inv_v, rhs_v, blk_v, pat_s,
    w_v, rhs_t, zsend, zrecv, fsend, frecv, esend, erecv, ysend, yrecv, csend, crecv, l_out, l_in, xz, acc, u_piece, u_all, f_all, prod,
    in_sem, zs_sem, zr_sem, fs_sem, fr_sem, es_sem, er_sem, cs_sem, cr_sem, ls_sem, lr_sem, vs_sem, vr_sem, ys_sem, yr_sem, xs_sem, xr_sem, us_sem, ur_sem, ws_sem, wr_sem, ds_sem, dr_sem,
):
    n_g, n_p, n_q, levels, width, n_b = dims
    g = lax.axis_index("gz")
    p = lax.axis_index("pr")
    q = lax.axis_index("pc")
    nb = n_p // n_q
    own = lax.rem(p, n_q) == q
    own_b = p // n_q

    part_rows = prod.shape[1]
    halves = width // part_rows

    rest = pl.ds(width, (levels - 1) * width)
    pairs = (
        (sub_hbm, sub_v),
        (low_hbm.at[pl.ds(0, width)], low_v.at[pl.ds(0, width)]),
        (low_hbm.at[rest], low_v.at[rest]),
        (blk_hbm, blk_v),
        (pat_hbm, pat_s),
        (inv_hbm, inv_v),
        (rhs_hbm, rhs_v),
        (up_hbm, up_v),
    )
    loads = [pltpu.make_async_copy(a, b, in_sem.at[k]) for k, (a, b) in enumerate(pairs)]
    for c in loads:
        c.start()

    def z_peer(r):
        return {"gz": lax.rem(g + r, n_g)}

    def x_peer(r):
        return {"pc": lax.rem(q + r, n_q)}

    def y_peer(r):
        return {"pr": lax.rem(p + r, n_p)}

    def cross_peer(b):
        return {"pr": b * n_q + q, "pc": lax.rem(p, n_q)}

    barrier = pltpu.get_barrier_semaphore()
    for r in ring_order(n_g):
        pl.semaphore_signal(barrier, inc=1, device_id=z_peer(r), device_id_type=MESH)
    for r in ring_order(n_p):
        pl.semaphore_signal(barrier, inc=1, device_id=y_peer(r), device_id_type=MESH)
    for r in ring_order(n_q):
        pl.semaphore_signal(barrier, inc=1, device_id=x_peer(r), device_id_type=MESH)

    @pl.when(jnp.logical_not(own))
    def _():
        for b in range(nb):
            pl.semaphore_signal(barrier, inc=1, device_id=cross_peer(b), device_id_type=MESH)

    def remote(src, dst, ssem, rsem, peer):
        return pltpu.make_async_remote_copy(
            src_ref=src, dst_ref=dst, send_sem=ssem, recv_sem=rsem, device_id=peer, device_id_type=MESH
        )

    sends = []

    def partial_update(a):
        part = jnp.dot(low_v[a * width : (a + 1) * width, :], sub_v[...], preferred_element_type=F32)
        flipped = jnp.transpose(part).astype(BF16)
        zsend[a] = flipped.reshape(n_g, flipped.shape[0] // n_g, width)

    def z_copy(a, r):
        return remote(
            zsend.at[a, lax.rem(g + r, n_g)], zrecv.at[a, r - 1], zs_sem.at[a, r - 1], zr_sem.at[a, r - 1], z_peer(r)
        )

    loads[0].wait()
    loads[1].wait()
    partial_update(0)
    pl.semaphore_wait(barrier, n_g + n_p + n_q - 3 + jnp.where(own, 0, nb))
    for r in ring_order(n_g):
        c = z_copy(0, r)
        c.start()
        sends.append(c)
    loads[2].wait()
    for a in range(1, levels):
        partial_update(a)
        for r in ring_order(n_g):
            c = z_copy(a, r)
            c.start()
            sends.append(c)

    def slot_of(row_level, col_level):
        return row_level * (levels - 1) + (col_level if col_level < row_level else col_level - 1)

    def masked_blocks(row_level, col_level):
        for b in range(nb):
            i = row_level * n_p + p
            j = col_level * n_p + b * n_q + q
            mark = pat_s[i, j] if col_level < row_level else pat_s[j, i]
            block = blk_v[row_level, col_level * nb + b]
            w_v[slot_of(row_level, col_level), :, b * width : (b + 1) * width] = jnp.where(
                mark == 1, block, jnp.zeros_like(block)
            )

    def weights(row_level, col_level):
        return w_v[slot_of(row_level, col_level)]

    def fold(level, col_level):
        slot = slot_of(level, col_level)
        w_v[slot] = jnp.dot(inv_v[level], w_v[slot], preferred_element_type=F32).astype(BF16)

    for k in (3, 4, 5):
        loads[k].wait()
    masked_blocks(2, 1)
    fold(2, 1)
    for b in range(nb):
        l_out[b] = w_v[slot_of(2, 1), :, b * width : (b + 1) * width]

    def l_copy(b):
        return remote(l_out.at[b], l_in.at[own_b], ls_sem.at[b], lr_sem.at[own_b], cross_peer(b))

    def l_arrival(b):
        return remote(l_out.at[b], l_in.at[b], ls_sem.at[b], lr_sem.at[b], cross_peer(b))

    for b in range(nb):

        @pl.when(b * n_q + q != p)
        def _(b=b):
            l_copy(b).start()

    @pl.when(own)
    def _():
        l_in[own_b] = l_out[own_b]

    first, second = slot_of(0, 1), slot_of(1, 2)
    masked_blocks(0, 1)
    masked_blocks(1, 2)

    def f_copy(r):
        return remote(w_v.at[first], f_all.at[r - 1], ws_sem.at[r - 1], wr_sem.at[r - 1], x_peer(r))

    def u_copy(r):
        return remote(u_piece.at[g % halves], u_all.at[p], us_sem.at[r - 1], ur_sem.at[r - 1], y_peer(r))

    def d_copy(r):
        return remote(prod.at[g], prod.at[g], ds_sem.at[r - 1], dr_sem.at[r - 1], z_peer(r))

    for r in ring_order(n_q):
        c = f_copy(r)
        c.start()
        sends.append(c)
    mine = w_v[second, :, pl.ds(pl.multiple_of(g // halves * width, width), width)]
    u_piece[...] = jnp.transpose(mine.astype(F32)).astype(BF16).reshape(halves, part_rows, width)
    for r in ring_order(n_p):
        c = u_copy(r)
        c.start()
        sends.append(c)
    u_all[p] = u_piece[g % halves]

    for row_level in range(1, levels):
        masked_blocks(row_level, 0)
        fold(row_level, 0)
    masked_blocks(0, 2)
    loads[6].wait()
    for a in range(levels):
        rhs_t[a] = jnp.transpose(rhs_v[a].astype(F32)).reshape(n_g, rhs_t.shape[2], width)

    def form_product():
        for r in range(1, n_p):
            u_copy(r).wait_recv()
        total = None
        for r in range(n_q):
            if r:
                f_copy(r).wait_recv()
            left = weights(0, 1) if r == 0 else f_all[r - 1]
            from_q = lax.rem(q + n_q - r, n_q)
            right = jnp.concatenate([u_all[b * n_q + from_q] for b in range(nb)], axis=1)
            term = nt(right, left)
            total = term if total is None else total + term
        prod[g] = total.astype(BF16)
        for r in ring_order(n_g):
            c = d_copy(r)
            c.start()
            sends.append(c)

    def product():
        for r in range(1, n_g):
            d_copy(r).wait_recv()
        return prod[...].reshape(n_g * part_rows, width)

    def z_total(a):
        for r in range(1, n_g):
            z_copy(a, r).wait_recv()
        total = zsend[a, g].astype(F32)
        for r in range(1, n_g):
            total = total + zrecv[a, r - 1].astype(F32)
        return total.astype(BF16)

    def exchange(value, src, dst, ssem, rsem):
        src[...] = value
        copies = []
        for r in ring_order(n_q):
            c = remote(src, dst.at[r - 1], ssem.at[r - 1], rsem.at[r - 1], x_peer(r))
            c.start()
            copies.append(c)
            sends.append(c)
        return copies

    def collected(value, copies, dst):
        for c in copies:
            c.wait_recv()
        half = n_q // 2
        total = None
        for k in range(half):
            first = value.astype(F32) if k == 0 else dst[k - 1].astype(F32)
            pair = first + dst[k + half - 1].astype(F32)
            total = pair if total is None else total + pair
        return total

    def f_exchange(a):
        value = z_total(a)
        return value, exchange(value, fsend.at[a], frecv.at[a], fs_sem.at[a], fr_sem.at[a])

    def fed(a, started):
        value, copies = started
        return rhs_t[a, g] - collected(value, copies, frecv.at[a])

    def y_copy(k, r):
        return remote(ysend.at[k], yrecv.at[k, own_b], ys_sem.at[k, r - 1], yr_sem.at[k, own_b], y_peer(r))

    def broadcast(k, value):
        ysend[k] = value

        @pl.when(own)
        def _():
            for r in ring_order(n_p):
                y_copy(k, r).start()
            yrecv[k, own_b] = value

    def gathered(k):
        for b in range(nb):

            @pl.when(b * n_q + q != p)
            def _(b=b):
                remote(ysend.at[k], yrecv.at[k, b], ys_sem.at[k, 0], yr_sem.at[k, b], y_peer(1)).wait_recv()

        return jnp.concatenate([yrecv[k, b] for b in range(nb)], axis=1)

    def spread_copy(lo, n, r):
        mine = xz.at[g, pl.ds(lo, n)]
        return remote(mine, mine, xs_sem.at[lo, r - 1], xr_sem.at[lo, r - 1], z_peer(r))

    def spread(lo, values):
        for k, value in enumerate(values):
            xz[g, lo + k] = value
        for r in ring_order(n_g):
            c = spread_copy(lo, max(len(values), 1), r)
            c.start()
            sends.append(c)

    def solve(a, resid):
        return nt(resid.astype(BF16), inv_v[a])

    started = f_exchange(0)
    y0 = solve(0, fed(0, started)).astype(BF16)
    broadcast(0, y0)
    later = [f_exchange(a) for a in (1, 2)]
    solved1, solved2 = [solve(a, fed(a, later[a - 1])) for a in (1, 2)]

    block0 = gathered(0)
    both = jnp.concatenate([nt(block0, weights(a, 0)) for a in (1, 2)], axis=1).astype(BF16)
    copies = exchange(both, esend.at[0], erecv.at[0], es_sem.at[0], er_sem.at[0])
    for b in range(nb):

        @pl.when(b * n_q + q != p)
        def _(b=b):
            l_arrival(b).wait_recv()

    step2 = l_in[...].reshape(nb * width, width)
    total = collected(both, copies, erecv.at[0])
    y1 = (solved1 - total[:, :width]).astype(BF16)
    terms = nt(y1, step2).astype(BF16)
    for b in range(nb):
        csend[b] = terms[:, b * width : (b + 1) * width]

    def c_copy(b):
        ahead = lax.rem(b * n_q + q + n_p - p, n_p) - 1
        return remote(csend.at[b], crecv.at[ahead], cs_sem.at[b], cr_sem.at[ahead], {"pr": b * n_q + q})

    for b in range(nb):

        @pl.when(b * n_q + q != p)
        def _(b=b):
            c_copy(b).start()

    broadcast(1, y1)
    form_product()
    block1 = gathered(1)
    part0 = nt(block1, weights(0, 1))

    def v_copy(r):
        mine = xz.at[g, levels - 1]
        return remote(mine, mine, vs_sem.at[r - 1], vr_sem, x_peer(r))

    @pl.when(own)
    def _():
        sum2 = csend[own_b].astype(F32)
        for r in range(1, n_p):
            remote(csend.at[0], crecv.at[r - 1], cs_sem.at[0], cr_sem.at[r - 1], y_peer(1)).wait_recv()
            sum2 = sum2 + crecv[r - 1].astype(F32)
        y2 = (solved2 - total[:, width:] - sum2).astype(BF16)
        ysend[2] = y2
        for r in ring_order(n_p):
            y_copy(2, r).start()
        yrecv[2, own_b] = y2
        xz[g, levels - 1] = y2
        for r in ring_order(n_q):
            v_copy(r).start()

    weights0 = product()
    block2 = gathered(2)
    part1 = nt(block2, weights(1, 2))
    part0 = part0 + nt(block2, weights(0, 2)) - jnp.dot(block2, weights0, preferred_element_type=F32)
    both = jnp.concatenate([part0, part1], axis=1).astype(BF16)
    copies = exchange(both, esend.at[1], erecv.at[1], es_sem.at[1], er_sem.at[1])

    @pl.when(jnp.logical_not(own))
    def _():
        v_copy(1).wait_recv()

    spread(2, [])
    total = collected(both, copies, erecv.at[1])
    x0 = (y0.astype(F32) - total[:, :width]).astype(BF16)
    x1 = (y1.astype(F32) - total[:, width:]).astype(BF16)
    early = list(sends)
    spread(0, [x0, x1])

    loads[7].wait()
    rows = res_v.shape[0]
    n_c = 4
    chunk = rows // n_c

    def full(a):
        return xz[:, a].reshape(n_g * xz.shape[2], width)

    for r in range(1, n_g):
        spread_copy(2, 1, r).wait_recv()
    x2 = full(2)
    for c in range(n_c):
        span = pl.ds(c * chunk, chunk)
        acc[span, :] = sub_v[span, :].astype(F32) - nt(up_v[span, 2 * width :], x2)
    x_v[2] = jnp.transpose(x2.astype(F32)).astype(BF16)

    for c in early:
        c.wait_send()

    for b in range(nb):

        @pl.when(b * n_q + q != p)
        def _(b=b):
            l_copy(b).wait_send()
            c_copy(b).wait_send()

    @pl.when(own)
    def _():
        for k in range(levels):
            for r in range(1, n_p):
                y_copy(k, r).wait_send()
        for r in range(1, n_q):
            v_copy(r).wait_send()

    for r in range(1, n_g):
        spread_copy(0, 2, r).wait_recv()
    x01 = jnp.concatenate([full(0), full(1)], axis=1)
    for c in range(n_c):
        span = pl.ds(c * chunk, chunk)
        res_v[span, :] = (acc[span, :] - nt(up_v[span, : 2 * width], x01)).astype(BF16)
    for a in range(2):
        x_v[a] = jnp.transpose(full(a).astype(F32)).astype(BF16)
    for c in sends[len(early) :]:
        c.wait_send()


def store_kernel(x_v, res_v, x_hbm, res_hbm, sem):
    copies = [pltpu.make_async_copy(res_v, res_hbm, sem.at[0]), pltpu.make_async_copy(x_v, x_hbm, sem.at[1])]
    for c in copies:
        c.start()
    for c in copies:
        c.wait()


def per_device(dims, sep_rhs, diag_inverse, off_blocks, pattern, sub_solution, couple_low, couple_up):
    n_g, n_p, n_q, levels, width, n_b = dims
    sub = sub_solution.reshape(sub_solution.shape[-2:])
    low = couple_low.reshape(couple_low.shape[-2:])
    up = couple_up.reshape(couple_up.shape[-2:])
    rhs = sep_rhs.reshape(sep_rhs.shape[1:])
    inv = diag_inverse.reshape(diag_inverse.shape[1:])
    blk = off_blocks.reshape(levels, n_b, width, width)
    rows, cols = sub.shape
    piece = cols // n_g
    nb = n_p // n_q
    dma = pltpu.SemaphoreType.DMA
    wc = nb * width // n_g
    vmem = pltpu.VMEM
    x, res = pl.pallas_call(
        functools.partial(kernel, dims),
        out_shape=(vmem(rhs.shape, BF16), vmem(sub.shape, BF16)),
        in_specs=[pl.BlockSpec(memory_space=pl.ANY)] * 7,
        out_specs=(pl.BlockSpec(memory_space=vmem),) * 2,
        scratch_shapes=[
            vmem(sub.shape, BF16),
            vmem(low.shape, BF16),
            vmem(up.shape, BF16),
            vmem(inv.shape, BF16),
            vmem(rhs.shape, BF16),
            vmem(blk.shape, BF16),
            pltpu.SMEM(pattern.shape, jnp.int32),
            vmem((levels * (levels - 1), width, nb * width), BF16),
            vmem((levels, n_g, piece, width), F32),
            vmem((levels, n_g, piece, width), BF16),
            vmem((levels, n_g - 1, piece, width), BF16),
            vmem((levels, piece, width), BF16),
            vmem((levels, n_q - 1, piece, width), BF16),
            vmem((2, piece, 2 * width), BF16),
            vmem((2, n_q - 1, piece, 2 * width), BF16),
            vmem((levels, piece, width), BF16),
            vmem((levels, nb, piece, width), BF16),
            vmem((nb, piece, width), BF16),
            vmem((n_p - 1, piece, width), BF16),
            vmem((nb, width, width), BF16),
            vmem((nb, width, width), BF16),
            vmem((n_g, levels, piece, width), BF16),
            vmem(sub.shape, F32),
            vmem((width // wc, wc, width), BF16),
            vmem((n_p, wc, width), BF16),
            vmem((n_q - 1, width, nb * width), BF16),
            vmem((n_g, wc, width), BF16),
            dma((8,)),
            dma((levels, n_g - 1)),
            dma((levels, n_g - 1)),
            dma((levels, n_q - 1)),
            dma((levels, n_q - 1)),
            dma((2, n_q - 1)),
            dma((2, n_q - 1)),
            dma((nb,)),
            dma((n_p - 1,)),
            dma((nb,)),
            dma((nb,)),
            dma((n_q - 1,)),
            dma(()),
            dma((levels, n_p - 1)),
            dma((levels, nb)),
            dma((levels, n_g - 1)),
            dma((levels, n_g - 1)),
            dma((n_p - 1,)),
            dma((n_p - 1,)),
            dma((n_q - 1,)),
            dma((n_q - 1,)),
            dma((n_g - 1,)),
            dma((n_g - 1,)),
        ],
        compiler_params=pltpu.CompilerParams(collective_id=0, has_side_effects=True),
    )(rhs, inv, blk, pattern, sub, low, up)
    x, res = pl.pallas_call(
        store_kernel,
        out_shape=(jax.ShapeDtypeStruct(rhs.shape, BF16), jax.ShapeDtypeStruct(sub.shape, BF16)),
        in_specs=[pl.BlockSpec(memory_space=vmem)] * 2,
        out_specs=(pl.BlockSpec(memory_space=pl.ANY),) * 2,
        scratch_shapes=[dma((2,))],
    )(*(pltpu.with_memory_space_constraint(v, vmem) for v in (x, res)))
    return x[None], res[None, None, None]


def solution(mesh):
    n_g, n_p, n_q = mesh.shape["gz"], mesh.shape["pr"], mesh.shape["pc"]

    def step(*args):
        levels, width = args[1].shape[1], args[1].shape[2]
        dims = (n_g, n_p, n_q, levels, width, args[2].shape[2])
        return per_device(dims, *args)

    return jax.shard_map(
        step,
        mesh=mesh,
        in_specs=(
            P("pr", None, None, None),
            P("pr", None, None, None),
            P("pr", None, None, "pc", None, None),
            P(),
            P("gz", "pr", "pc", None, None),
            P("gz", "pr", "pc", None, None),
            P("gz", "pr", "pc", None, None),
        ),
        out_specs=(P("pr", None, None, None), P("gz", "pr", "pc", None, None)),
        check_vma=False,
    )
```

```python
import functools

import jax
import jax.numpy as jnp
from jax import lax
from jax.experimental import pallas as pl
from jax.experimental.pallas import tpu as pltpu
from jax.sharding import PartitionSpec as P

F32 = jnp.float32
BF16 = jnp.bfloat16
MESH = pl.DeviceIdType.MESH


def nt(a, b):
    return lax.dot_general(a, b, (((1,), (1,)), ((), ())), preferred_element_type=F32)


def ring_order(n):
    return sorted(range(1, n), key=lambda r: (-min(r, n - r), r))


def kernel(
    dims,
    rhs_hbm, inv_hbm, blk_hbm, pat_hbm, sub_hbm, low_hbm, up_hbm,
    x_out, acc, up01_v,
    sub_v, low_v, up2_v, inv_v, rhs_v, blk_v, pat_s,
    w_v, wl_v, wu_v, rhs_t, zsend, zrecv, fsend, frecv, esend, erecv, ysend, yrecv, csend, crecv, l_out, l_in, xz, u_piece, u_all, f_all, prod,
    in_sem, zs_sem, zr_sem, fs_sem, fr_sem, es_sem, er_sem, cs_sem, cr_sem, ls_sem, lr_sem, vs_sem, vr_sem, ys_sem, yr_sem, xs_sem, xr_sem, us_sem, ur_sem, ws_sem, wr_sem, ds_sem, dr_sem,
):
    n_g, n_p, n_q, levels, width, n_b = dims
    g = lax.axis_index("gz")
    p = lax.axis_index("pr")
    q = lax.axis_index("pc")
    nb = n_p // n_q
    own = lax.rem(p, n_q) == q
    own_b = p // n_q

    part_rows = prod.shape[1]
    halves = width // part_rows

    rest = pl.ds(width, (levels - 1) * width)
    pairs = (
        (sub_hbm, sub_v),
        (low_hbm.at[pl.ds(0, width)], low_v.at[pl.ds(0, width)]),
        (low_hbm.at[rest], low_v.at[rest]),
        (blk_hbm, blk_v),
        (pat_hbm, pat_s),
        (inv_hbm, inv_v),
        (rhs_hbm, rhs_v),
        (up_hbm.at[:, pl.ds(2 * width, width)], up2_v),
        (up_hbm.at[:, pl.ds(0, 2 * width)], up01_v),
    )
    loads = [pltpu.make_async_copy(a, b, in_sem.at[k]) for k, (a, b) in enumerate(pairs)]
    for c in loads:
        c.start()

    def z_peer(r):
        return {"gz": lax.rem(g + r, n_g)}

    def x_peer(r):
        return {"pc": lax.rem(q + r, n_q)}

    def y_peer(r):
        return {"pr": lax.rem(p + r, n_p)}

    def cross_peer(b):
        return {"pr": b * n_q + q, "pc": lax.rem(p, n_q)}

    barrier = pltpu.get_barrier_semaphore()
    for r in ring_order(n_g):
        pl.semaphore_signal(barrier, inc=1, device_id=z_peer(r), device_id_type=MESH)
    for r in ring_order(n_p):
        pl.semaphore_signal(barrier, inc=1, device_id=y_peer(r), device_id_type=MESH)
    for r in ring_order(n_q):
        pl.semaphore_signal(barrier, inc=1, device_id=x_peer(r), device_id_type=MESH)

    @pl.when(jnp.logical_not(own))
    def _():
        for b in range(nb):
            pl.semaphore_signal(barrier, inc=1, device_id=cross_peer(b), device_id_type=MESH)

    def remote(src, dst, ssem, rsem, peer):
        return pltpu.make_async_remote_copy(
            src_ref=src, dst_ref=dst, send_sem=ssem, recv_sem=rsem, device_id=peer, device_id_type=MESH
        )

    drains = []

    def send_all(copies, size, sem):
        for c in copies:
            c.start()
        drains.append((size, sem))

    def sent(size, sem):
        remote(size, size, sem, sem, x_peer(1)).wait_send()

    def arrived(size, sem):
        remote(size, size, sem, sem, x_peer(1)).wait_recv()

    def fewer_if_own(wait, ref, sem):
        @pl.when(own)
        def _():
            wait(ref.at[pl.ds(0, nb - 1)], sem)

        @pl.when(jnp.logical_not(own))
        def _():
            wait(ref, sem)


    def partial_update(a):
        part = jnp.dot(low_v[a * width : (a + 1) * width, :], sub_v[...], preferred_element_type=F32)
        flipped = jnp.transpose(part).astype(BF16)
        zsend[a] = flipped.reshape(n_g, flipped.shape[0] // n_g, width)

    def z_copy(a, r):
        k = min(a, 1)
        return remote(zsend.at[a, lax.rem(g + r, n_g)], zrecv.at[a, r - 1], zs_sem.at[k], zr_sem.at[k], z_peer(r))

    others = pl.ds(1, levels - 1)

    loads[0].wait()
    loads[1].wait()
    partial_update(0)

    def slot_of(row_level, col_level):
        return row_level * (levels - 1) + (col_level if col_level < row_level else col_level - 1)

    def masked_blocks(row_level, col_level):
        for b in range(nb):
            i = row_level * n_p + p
            j = col_level * n_p + b * n_q + q
            mark = pat_s[i, j] if col_level < row_level else pat_s[j, i]
            block = blk_v[row_level, col_level * nb + b]
            w_v[slot_of(row_level, col_level), :, b * width : (b + 1) * width] = jnp.where(
                mark == 1, block, jnp.zeros_like(block)
            )

    def weights(row_level, col_level):
        return w_v[slot_of(row_level, col_level)]

    def folded(level, col_level):
        return jnp.dot(inv_v[level], weights(level, col_level), preferred_element_type=F32).astype(BF16)

    for k in (3, 4, 5):
        loads[k].wait()
    masked_blocks(2, 1)
    step21 = folded(2, 1)
    for b in range(nb):
        l_out[b] = step21[:, b * width : (b + 1) * width]

    def l_copy(b):
        return remote(l_out.at[b], l_in.at[own_b], ls_sem, lr_sem, cross_peer(b))

    @pl.when(own)
    def _():
        l_in[own_b] = l_out[own_b]

    first, second = slot_of(0, 1), slot_of(1, 2)
    masked_blocks(0, 1)
    masked_blocks(1, 2)

    def f_copy(h, r):
        span = pl.ds(h * (nb * width // 2), nb * width // 2)
        return remote(w_v.at[first, :, span], f_all.at[r - 1, :, span], ws_sem, wr_sem, x_peer(r))

    def f_send(h):
        for r in ring_order(n_q):
            f_copy(h, r).start()

    def u_copy(r):
        return remote(u_piece.at[g % halves], u_all.at[p], us_sem, ur_sem, y_peer(r))

    def d_copy(r):
        return remote(prod.at[g], prod.at[g], ds_sem, dr_sem, z_peer(r))

    mine = w_v[second, :, pl.ds(pl.multiple_of(g // halves * width, width), width)]
    u_piece[...] = jnp.transpose(mine.astype(F32)).astype(BF16).reshape(halves, part_rows, width)
    u_all[p] = u_piece[g % halves]

    pl.semaphore_wait(barrier, n_g + n_p + n_q - 3 + jnp.where(own, 0, nb))
    send_all([z_copy(0, r) for r in ring_order(n_g)], zrecv.at[0], zs_sem.at[0])
    f_send(0)
    for b in range(nb):

        @pl.when(b * n_q + q != p)
        def _(b=b):
            l_copy(b).start()

    send_all([u_copy(r) for r in ring_order(n_p)], u_all.at[pl.ds(0, n_p - 1)], us_sem)
    loads[2].wait()
    for a in range(1, levels):
        partial_update(a)
        for r in ring_order(n_g):
            z_copy(a, r).start()
    drains.append((zrecv.at[others], zs_sem.at[1]))

    for row_level in range(1, levels):
        masked_blocks(row_level, 0)
        wl_v[(row_level - 1) * width : row_level * width, :] = folded(row_level, 0)
    masked_blocks(0, 2)
    for k, w in enumerate((weights(0, 2), weights(1, 2))):
        wu_v[:, k * width : (k + 1) * width] = jnp.transpose(w.astype(F32)).astype(BF16)
    loads[6].wait()
    for a in range(levels):
        rhs_t[a] = jnp.transpose(rhs_v[a].astype(F32)).reshape(n_g, rhs_t.shape[2], width)

    def form_product():
        arrived(u_all.at[pl.ds(0, n_p - 1)], ur_sem)
        arrived(f_all, wr_sem)
        total = None
        for r in range(n_q):
            left = weights(0, 1) if r == 0 else f_all[r - 1]
            from_q = lax.rem(q + n_q - r, n_q)
            right = jnp.concatenate([u_all[b * n_q + from_q] for b in range(nb)], axis=1)
            term = nt(right, left)
            total = term if total is None else total + term
        prod[g] = total.astype(BF16)
        send_all([d_copy(r) for r in ring_order(n_g)], prod.at[pl.ds(0, n_g - 1)], ds_sem)

    def product():
        arrived(prod.at[pl.ds(0, n_g - 1)], dr_sem)
        return prod[...].reshape(n_g * part_rows, width)

    def z_total(a):
        total = zsend[a, g].astype(F32)
        for r in range(1, n_g):
            total = total + zrecv[a, r - 1].astype(F32)
        return total.astype(BF16)

    def exchange(value, src, dst, ssem, rsem):
        src[...] = value
        send_all([remote(src, dst.at[r - 1], ssem, rsem, x_peer(r)) for r in ring_order(n_q)], dst, ssem)

    def collected(value, dst, rsem):
        arrived(dst, rsem)
        half = n_q // 2
        total = None
        for k in range(half):
            start = value.astype(F32) if k == 0 else dst[k - 1].astype(F32)
            pair = start + dst[k + half - 1].astype(F32)
            total = pair if total is None else total + pair
        return total

    def y_copy(k, r):
        return remote(ysend.at[k], yrecv.at[k, own_b], ys_sem.at[k], yr_sem.at[k], y_peer(r))

    def broadcast_own(k, value):
        ysend[k] = value
        for r in ring_order(n_p):
            y_copy(k, r).start()
        yrecv[k, own_b] = value

    def gathered(k):
        fewer_if_own(arrived, yrecv.at[k], yr_sem.at[k])
        return jnp.concatenate([yrecv[k, b] for b in range(nb)], axis=1)

    def spread(k, lo, n):
        mine = xz.at[g, pl.ds(lo, n)]
        copies = [remote(mine, mine, xs_sem.at[k], xr_sem.at[k], z_peer(r)) for r in ring_order(n_g)]
        send_all(copies, zrecv.at[pl.ds(lo, n)], xs_sem.at[k])

    def solve(a, resid):
        return nt(resid.astype(BF16), inv_v[a])

    arrived(zrecv.at[0], zr_sem.at[0])
    value = z_total(0)
    exchange(value, fsend, frecv, fs_sem, fr_sem)
    y0 = solve(0, rhs_t[0, g] - collected(value, frecv, fr_sem)).astype(BF16)

    @pl.when(own)
    def _():
        broadcast_own(0, y0)

    arrived(zrecv.at[others], zr_sem.at[1])
    both = jnp.concatenate([z_total(a) for a in (1, 2)], axis=1)
    exchange(both, esend.at[0], erecv.at[0], es_sem.at[0], er_sem.at[0])
    f_send(1)
    drains.append((f_all, ws_sem))
    total = collected(both, erecv.at[0], er_sem.at[0])
    solved1 = solve(1, rhs_t[1, g] - total[:, :width])
    solved2 = solve(2, rhs_t[2, g] - total[:, width:])

    both = nt(gathered(0), wl_v[...]).astype(BF16)
    exchange(both, esend.at[1], erecv.at[1], es_sem.at[1], er_sem.at[1])
    fewer_if_own(arrived, l_in, lr_sem)
    step2 = l_in[...].reshape(nb * width, width)
    total = collected(both, erecv.at[1], er_sem.at[1])
    y1 = (solved1 - total[:, :width]).astype(BF16)
    rest2 = solved2 - total[:, width:]
    terms = nt(y1, step2).astype(BF16)
    for b in range(nb):
        csend[b] = terms[:, b * width : (b + 1) * width]
    for b in range(nb):

        @pl.when(b * n_q + q != p)
        def _(b=b):
            ahead = lax.rem(b * n_q + q + n_p - p, n_p) - 1
            remote(csend.at[b], crecv.at[ahead], cs_sem, cr_sem, {"pr": b * n_q + q}).start()

    @pl.when(own)
    def _():
        broadcast_own(1, y1)

    form_product()

    @pl.when(own)
    def _():
        arrived(crecv, cr_sem)
        sum2 = csend[own_b].astype(F32)
        for r in range(1, n_p):
            sum2 = sum2 + crecv[r - 1].astype(F32)
        y2 = (rest2 - sum2).astype(BF16)
        broadcast_own(2, y2)
        mine = xz.at[g, levels - 1]
        mine[...] = y2
        for r in ring_order(n_q):
            remote(mine, mine, vs_sem, vr_sem, x_peer(r)).start()

    part0 = nt(gathered(1), weights(0, 1))
    weights0 = product()
    wu_v[:, :width] = (wu_v[:, :width].astype(F32) - weights0.astype(F32)).astype(BF16)
    both = jnp.dot(gathered(2), wu_v[...], preferred_element_type=F32)
    both = jnp.concatenate([both[:, :width] + part0, both[:, width:]], axis=1).astype(BF16)
    exchange(both, esend.at[2], erecv.at[2], es_sem.at[2], er_sem.at[2])

    @pl.when(jnp.logical_not(own))
    def _():
        arrived(xz.at[g, levels - 1], vr_sem)

    spread(0, levels - 1, 1)
    total = collected(both, erecv.at[2], er_sem.at[2])
    xz[g, 0] = (y0.astype(F32) - total[:, :width]).astype(BF16)
    xz[g, 1] = (y1.astype(F32) - total[:, width:]).astype(BF16)
    early = list(drains)
    spread(1, 0, 2)

    loads[7].wait()
    rows = acc.shape[0]
    n_c = 4
    chunk = rows // n_c

    def full(a):
        return xz[:, a].reshape(n_g * xz.shape[2], width)

    arrived(zrecv.at[0], xr_sem.at[0])
    x2 = full(2)
    for c in range(n_c):
        span = pl.ds(c * chunk, chunk)
        acc[span, :] = sub_v[span, :].astype(F32) - nt(up2_v[span, :], x2)
    x_out[:, 2 * width :] = x2
    loads[8].wait()
    for size, sem in early:
        sent(size, sem)
    fewer_if_own(sent, l_in, ls_sem)
    fewer_if_own(sent, csend, cs_sem)

    @pl.when(own)
    def _():
        for k in range(levels):
            sent(crecv, ys_sem.at[k])
        sent(frecv, vs_sem)

    arrived(zrecv.at[pl.ds(0, 2)], xr_sem.at[1])
    for a in range(2):
        x_out[:, a * width : (a + 1) * width] = full(a)
    for size, sem in drains[len(early) :]:
        sent(size, sem)


def store_kernel(xt_v, acc, up01_v, x_hbm, res_hbm, x_v, res_v, sem):
    levels, width = x_v.shape[0], x_v.shape[1]
    n_c = 4
    chunk = acc.shape[0] // n_c
    copies = []
    x01 = xt_v[:, : 2 * width]
    for c in range(n_c):
        span = pl.ds(c * chunk, chunk)
        res_v[span, :] = (acc[span, :] - nt(up01_v[span, :], x01)).astype(BF16)
        copies.append(pltpu.make_async_copy(res_v.at[span], res_hbm.at[span], sem.at[c]))
        copies[-1].start()
    for a in range(levels):
        x_v[a] = jnp.transpose(xt_v[:, a * width : (a + 1) * width].astype(F32)).astype(BF16)
    copies.append(pltpu.make_async_copy(x_v, x_hbm, sem.at[n_c]))
    copies[-1].start()
    for c in copies:
        c.wait()


def per_device(dims, sep_rhs, diag_inverse, off_blocks, pattern, sub_solution, couple_low, couple_up):
    n_g, n_p, n_q, levels, width, n_b = dims
    sub = sub_solution.reshape(sub_solution.shape[-2:])
    low = couple_low.reshape(couple_low.shape[-2:])
    up = couple_up.reshape(couple_up.shape[-2:])
    rhs = sep_rhs.reshape(sep_rhs.shape[1:])
    inv = diag_inverse.reshape(diag_inverse.shape[1:])
    blk = off_blocks.reshape(levels, n_b, width, width)
    rows, cols = sub.shape
    piece = cols // n_g
    nb = n_p // n_q
    dma = pltpu.SemaphoreType.DMA
    wc = nb * width // n_g
    vmem = pltpu.VMEM
    xt, acc, up01 = pl.pallas_call(
        functools.partial(kernel, dims),
        out_shape=(vmem((cols, levels * width), BF16), vmem(sub.shape, F32), vmem((rows, 2 * width), BF16)),
        in_specs=[pl.BlockSpec(memory_space=pl.ANY)] * 7,
        out_specs=(pl.BlockSpec(memory_space=vmem),) * 3,
        scratch_shapes=[
            vmem(sub.shape, BF16),
            vmem(low.shape, BF16),
            vmem((rows, width), BF16),
            vmem(inv.shape, BF16),
            vmem(rhs.shape, BF16),
            vmem(blk.shape, BF16),
            pltpu.SMEM(pattern.shape, jnp.int32),
            vmem((levels * (levels - 1), width, nb * width), BF16),
            vmem((2 * width, nb * width), BF16),
            vmem((nb * width, 2 * width), BF16),
            vmem((levels, n_g, piece, width), F32),
            vmem((levels, n_g, piece, width), BF16),
            vmem((levels, n_g - 1, piece, width), BF16),
            vmem((piece, width), BF16),
            vmem((n_q - 1, piece, width), BF16),
            vmem((3, piece, 2 * width), BF16),
            vmem((3, n_q - 1, piece, 2 * width), BF16),
            vmem((levels, piece, width), BF16),
            vmem((levels, nb, piece, width), BF16),
            vmem((nb, piece, width), BF16),
            vmem((n_p - 1, piece, width), BF16),
            vmem((nb, width, width), BF16),
            vmem((nb, width, width), BF16),
            vmem((n_g, levels, piece, width), BF16),
            vmem((width // wc, wc, width), BF16),
            vmem((n_p, wc, width), BF16),
            vmem((n_q - 1, width, nb * width), BF16),
            vmem((n_g, wc, width), BF16),
            dma((9,)),
            dma((2,)),
            dma((2,)),
            dma(()),
            dma(()),
            dma((3,)),
            dma((3,)),
            dma(()),
            dma(()),
            dma(()),
            dma(()),
            dma(()),
            dma(()),
            dma((levels,)),
            dma((levels,)),
            dma((2,)),
            dma((2,)),
            dma(()),
            dma(()),
            dma(()),
            dma(()),
            dma(()),
            dma(()),
        ],
        compiler_params=pltpu.CompilerParams(collective_id=0, has_side_effects=True),
    )(rhs, inv, blk, pattern, sub, low, up)
    x, res = pl.pallas_call(
        store_kernel,
        out_shape=(jax.ShapeDtypeStruct(rhs.shape, BF16), jax.ShapeDtypeStruct(sub.shape, BF16)),
        in_specs=[pl.BlockSpec(memory_space=vmem)] * 3,
        out_specs=(pl.BlockSpec(memory_space=pl.ANY),) * 2,
        scratch_shapes=[vmem(rhs.shape, BF16), vmem(sub.shape, BF16), dma((5,))],
    )(*(pltpu.with_memory_space_constraint(v, vmem) for v in (xt, acc, up01)))
    return x[None], res[None, None, None]


def solution(mesh):
    n_g, n_p, n_q = mesh.shape["gz"], mesh.shape["pr"], mesh.shape["pc"]

    def step(*args):
        levels, width = args[1].shape[1], args[1].shape[2]
        dims = (n_g, n_p, n_q, levels, width, args[2].shape[2])
        return per_device(dims, *args)

    return jax.shard_map(
        step,
        mesh=mesh,
        in_specs=(
            P("pr", None, None, None),
            P("pr", None, None, None),
            P("pr", None, None, "pc", None, None),
            P(),
            P("gz", "pr", "pc", None, None),
            P("gz", "pr", "pc", None, None),
            P("gz", "pr", "pc", None, None),
        ),
        out_specs=(P("pr", None, None, None), P("gz", "pr", "pc", None, None)),
        check_vma=False,
    )
```

```python
import functools

import jax
import jax.numpy as jnp
from jax import lax
from jax.experimental import pallas as pl
from jax.experimental.pallas import tpu as pltpu
from jax.sharding import PartitionSpec as P

F32 = jnp.float32
BF16 = jnp.bfloat16
MESH = pl.DeviceIdType.MESH


def nt(a, b):
    return lax.dot_general(a, b, (((1,), (1,)), ((), ())), preferred_element_type=F32)


def ring_order(n):
    return sorted(range(1, n), key=lambda r: (-min(r, n - r), r))


def kernel(
    dims,
    rhs_hbm, inv_hbm, blk_hbm, pat_hbm, sub_hbm, low_hbm, up_hbm,
    x_out, acc, up01_v,
    sub_v, low_v, up2_v, inv_v, rhs_v, blk_v, pat_s,
    w_v, wl_v, wu_v, inv_t, rhs_t, zsend, zrecv, fsend, frecv, esend, erecv, ysend, yrecv, csend, crecv, l_out, l_in, xz, u_piece, u_all, f_all, prod,
    in_sem, zs_sem, zr_sem, fs_sem, fr_sem, es_sem, er_sem, cs_sem, cr_sem, ls_sem, lr_sem, vs_sem, vr_sem, ys_sem, yr_sem, xs_sem, xr_sem, us_sem, ur_sem, ws_sem, wr_sem, ds_sem, dr_sem,
):
    n_g, n_p, n_q, levels, width, n_b = dims
    g = lax.axis_index("gz")
    p = lax.axis_index("pr")
    q = lax.axis_index("pc")
    nb = n_p // n_q
    own = lax.rem(p, n_q) == q
    own_b = p // n_q

    part_rows = prod.shape[1]
    halves = width // part_rows

    rest = pl.ds(width, (levels - 1) * width)
    pairs = (
        (sub_hbm, sub_v),
        (low_hbm.at[pl.ds(0, width)], low_v.at[pl.ds(0, width)]),
        (low_hbm.at[rest], low_v.at[rest]),
        (blk_hbm, blk_v),
        (pat_hbm, pat_s),
        (inv_hbm, inv_v),
        (rhs_hbm, rhs_v),
        (up_hbm.at[:, pl.ds(2 * width, width)], up2_v),
        (up_hbm.at[:, pl.ds(0, 2 * width)], up01_v),
    )
    loads = [pltpu.make_async_copy(a, b, in_sem.at[k]) for k, (a, b) in enumerate(pairs)]
    for c in loads:
        c.start()

    def z_peer(r):
        return {"gz": lax.rem(g + r, n_g)}

    def x_peer(r):
        return {"pc": lax.rem(q + r, n_q)}

    def y_peer(r):
        return {"pr": lax.rem(p + r, n_p)}

    def cross_peer(b):
        return {"pr": b * n_q + q, "pc": lax.rem(p, n_q)}

    barrier = pltpu.get_barrier_semaphore()
    @pl.when(jnp.logical_not(own))
    def _():
        for b in range(nb):
            pl.semaphore_signal(barrier, inc=1, device_id=cross_peer(b), device_id_type=MESH)

    for r in ring_order(n_g):
        pl.semaphore_signal(barrier, inc=1, device_id=z_peer(r), device_id_type=MESH)
    for r in ring_order(n_p):
        pl.semaphore_signal(barrier, inc=1, device_id=y_peer(r), device_id_type=MESH)
    for r in ring_order(n_q):
        pl.semaphore_signal(barrier, inc=1, device_id=x_peer(r), device_id_type=MESH)

    def remote(src, dst, ssem, rsem, peer):
        return pltpu.make_async_remote_copy(
            src_ref=src, dst_ref=dst, send_sem=ssem, recv_sem=rsem, device_id=peer, device_id_type=MESH
        )

    drains = []

    def send_all(copies, size, sem):
        for c in copies:
            c.start()
        drains.append((size, sem))

    def sent(size, sem):
        remote(size, size, sem, sem, x_peer(1)).wait_send()

    def arrived(size, sem):
        remote(size, size, sem, sem, x_peer(1)).wait_recv()

    def fewer_if_own(wait, ref, sem):
        @pl.when(own)
        def _():
            wait(ref.at[pl.ds(0, nb - 1)], sem)

        @pl.when(jnp.logical_not(own))
        def _():
            wait(ref, sem)


    def partial_update(a):
        part = jnp.dot(low_v[a * width : (a + 1) * width, :], sub_v[...], preferred_element_type=F32)
        turned = jnp.transpose(part).astype(BF16)
        zsend[a] = turned.reshape(n_g, turned.shape[0] // n_g, width)

    def z_copy(a, r):
        k = min(a, 1)
        return remote(zsend.at[a, lax.rem(g + r, n_g)], zrecv.at[a, r - 1], zs_sem.at[k], zr_sem.at[k], z_peer(r))

    others = pl.ds(1, levels - 1)

    loads[0].wait()
    loads[1].wait()
    partial_update(0)

    def slot_of(row_level, col_level):
        return row_level * (levels - 1) + (col_level if col_level < row_level else col_level - 1)

    def masked_blocks(row_level, col_level):
        for b in range(nb):
            i = row_level * n_p + p
            j = col_level * n_p + b * n_q + q
            mark = pat_s[i, j] if col_level < row_level else pat_s[j, i]
            block = blk_v[row_level, col_level * nb + b]
            w_v[slot_of(row_level, col_level), :, b * width : (b + 1) * width] = jnp.where(
                mark == 1, block, jnp.zeros_like(block)
            )

    def weights(row_level, col_level):
        return w_v[slot_of(row_level, col_level)]

    def folded(level, col_level):
        return jnp.dot(inv_v[level], weights(level, col_level), preferred_element_type=F32)

    def flipped(a):
        return jnp.transpose(a.astype(F32)).astype(BF16)

    for k in (3, 4, 5):
        loads[k].wait()
    masked_blocks(2, 1)
    step21 = folded(2, 1)
    for b in range(nb):
        l_out[b] = flipped(step21[:, b * width : (b + 1) * width])

    def l_copy(b):
        return remote(l_out.at[b], l_in.at[own_b], ls_sem, lr_sem, cross_peer(b))

    @pl.when(own)
    def _():
        l_in[own_b] = l_out[own_b]

    first, second = slot_of(0, 1), slot_of(1, 2)
    masked_blocks(0, 1)
    masked_blocks(1, 2)

    def f_copy(h, r):
        span = pl.ds(h * (nb * width // 2), nb * width // 2)
        return remote(w_v.at[first, :, span], f_all.at[r - 1, :, span], ws_sem, wr_sem, x_peer(r))

    def f_send(h):
        for r in ring_order(n_q):
            f_copy(h, r).start()

    def u_copy(r):
        return remote(u_piece.at[g % halves], u_all.at[p], us_sem, ur_sem, y_peer(r))

    def d_copy(r):
        return remote(prod.at[g], prod.at[g], ds_sem, dr_sem, z_peer(r))

    mine = w_v[second, :, pl.ds(pl.multiple_of(g // halves * width, width), width)]
    u_piece[...] = jnp.transpose(mine.astype(F32)).astype(BF16).reshape(halves, part_rows, width)
    u_all[p] = u_piece[g % halves]

    pl.semaphore_wait(barrier, n_g + n_p + n_q - 3 + jnp.where(own, 0, nb))
    send_all([z_copy(0, r) for r in ring_order(n_g)], zrecv.at[0], zs_sem.at[0])
    f_send(0)
    for b in range(nb):

        @pl.when(b * n_q + q != p)
        def _(b=b):
            l_copy(b).start()

    send_all([u_copy(r) for r in ring_order(n_p)], u_all.at[pl.ds(0, n_p - 1)], us_sem)
    loads[2].wait()
    for a in range(1, levels):
        partial_update(a)
        for r in ring_order(n_g):
            z_copy(a, r).start()
    drains.append((zrecv.at[others], zs_sem.at[1]))

    for row_level in range(1, levels):
        masked_blocks(row_level, 0)
        wl_v[:, (row_level - 1) * width : row_level * width] = flipped(folded(row_level, 0))
    masked_blocks(0, 2)
    for k, w in enumerate((weights(0, 2), weights(1, 2))):
        wu_v[:, k * width : (k + 1) * width] = flipped(w)
    inv_t[...] = flipped(inv_v[0])
    loads[6].wait()
    for a in range(levels):
        rhs_t[a] = jnp.transpose(rhs_v[a].astype(F32)).reshape(n_g, rhs_t.shape[2], width)

    def form_product():
        arrived(u_all.at[pl.ds(0, n_p - 1)], ur_sem)
        arrived(f_all, wr_sem)
        total = None
        for r in range(n_q):
            left = weights(0, 1) if r == 0 else f_all[r - 1]
            from_q = lax.rem(q + n_q - r, n_q)
            right = jnp.concatenate([u_all[b * n_q + from_q] for b in range(nb)], axis=1)
            term = nt(right, left)
            total = term if total is None else total + term
        prod[g] = total.astype(BF16)
        send_all([d_copy(r) for r in ring_order(n_g)], prod.at[pl.ds(0, n_g - 1)], ds_sem)

    def product():
        arrived(prod.at[pl.ds(0, n_g - 1)], dr_sem)
        return prod[...].reshape(n_g * part_rows, width)

    def z_total(a):
        total = zsend[a, g].astype(F32)
        for r in range(1, n_g):
            total = total + zrecv[a, r - 1].astype(F32)
        return total.astype(BF16)

    def exchange(value, src, dst, ssem, rsem):
        src[...] = value
        send_all([remote(src, dst.at[r - 1], ssem, rsem, x_peer(r)) for r in ring_order(n_q)], dst, ssem)

    def collected(value, dst, rsem):
        arrived(dst, rsem)
        half = n_q // 2
        total = None
        for k in range(half):
            start = value.astype(F32) if k == 0 else dst[k - 1].astype(F32)
            pair = start + dst[k + half - 1].astype(F32)
            total = pair if total is None else total + pair
        return total

    def y_copy(k, r):
        return remote(ysend.at[k], yrecv.at[k, own_b], ys_sem.at[k], yr_sem.at[k], y_peer(r))

    def broadcast_own(k, value):
        ysend[k] = value
        for r in ring_order(n_p):
            y_copy(k, r).start()
        yrecv[k, own_b] = value

    def gathered(k):
        fewer_if_own(arrived, yrecv.at[k], yr_sem.at[k])
        return jnp.concatenate([yrecv[k, b] for b in range(nb)], axis=1)

    def solve(a, resid):
        return nt(resid.astype(BF16), inv_v[a])

    arrived(zrecv.at[0], zr_sem.at[0])
    value = z_total(0)
    exchange(value, fsend, frecv, fs_sem, fr_sem)
    resid = (rhs_t[0, g] - collected(value, frecv, fr_sem)).astype(BF16)
    y0 = jnp.dot(resid, inv_t[...], preferred_element_type=F32).astype(BF16)

    @pl.when(own)
    def _():
        broadcast_own(0, y0)

    arrived(zrecv.at[others], zr_sem.at[1])
    both = jnp.concatenate([z_total(a) for a in (1, 2)], axis=1)
    exchange(both, esend.at[0], erecv.at[0], es_sem.at[0], er_sem.at[0])
    f_send(1)
    drains.append((f_all, ws_sem))
    total = collected(both, erecv.at[0], er_sem.at[0])
    solved1 = solve(1, rhs_t[1, g] - total[:, :width])
    solved2 = solve(2, rhs_t[2, g] - total[:, width:])

    both = jnp.dot(gathered(0), wl_v[...], preferred_element_type=F32).astype(BF16)
    exchange(both, esend.at[1], erecv.at[1], es_sem.at[1], er_sem.at[1])
    fewer_if_own(arrived, l_in, lr_sem)
    step2 = jnp.concatenate([l_in[b] for b in range(nb)], axis=1)
    total = collected(both, erecv.at[1], er_sem.at[1])
    y1 = (solved1 - total[:, :width]).astype(BF16)
    rest2 = solved2 - total[:, width:]
    terms = jnp.dot(y1, step2, preferred_element_type=F32).astype(BF16)
    for b in range(nb):
        csend[b] = terms[:, b * width : (b + 1) * width]
    for b in range(nb):

        @pl.when(b * n_q + q != p)
        def _(b=b):
            ahead = lax.rem(b * n_q + q + n_p - p, n_p) - 1
            remote(csend.at[b], crecv.at[ahead], cs_sem, cr_sem, {"pr": b * n_q + q}).start()

    @pl.when(own)
    def _():
        broadcast_own(1, y1)

    form_product()

    @pl.when(own)
    def _():
        arrived(crecv, cr_sem)
        sum2 = csend[own_b].astype(F32)
        for r in range(1, n_p):
            sum2 = sum2 + crecv[r - 1].astype(F32)
        y2 = (rest2 - sum2).astype(BF16)
        broadcast_own(2, y2)
        mine = xz.at[g, levels - 1]
        mine[...] = y2
        for r in ring_order(n_q):
            remote(mine, mine, vs_sem, vr_sem, x_peer(r)).start()

    part0 = nt(gathered(1), weights(0, 1))
    weights0 = product()
    wu_v[:, :width] = (wu_v[:, :width].astype(F32) - weights0.astype(F32)).astype(BF16)
    both = jnp.dot(gathered(2), wu_v[...], preferred_element_type=F32)
    both = jnp.concatenate([both[:, :width] + part0, both[:, width:]], axis=1).astype(BF16)
    exchange(both, esend.at[2], erecv.at[2], es_sem.at[2], er_sem.at[2])

    @pl.when(jnp.logical_not(own))
    def _():
        arrived(xz.at[g, levels - 1], vr_sem)

    last = xz.at[g, pl.ds(levels - 1, 1)]
    copies = [remote(last, last, xs_sem.at[0], xr_sem.at[0], z_peer(r)) for r in ring_order(n_g)]
    send_all(copies, zrecv.at[pl.ds(0, 1)], xs_sem.at[0])
    total = collected(both, erecv.at[2], er_sem.at[2])
    xz[g, 0] = (y0.astype(F32) - total[:, :width]).astype(BF16)
    xz[g, 1] = (y1.astype(F32) - total[:, width:]).astype(BF16)
    early = list(drains)
    mine = xz.at[g, pl.ds(0, 2)]
    for plane in range(n_g):

        @pl.when(g != plane)
        def _(plane=plane):
            remote(mine, mine, xs_sem.at[1], xr_sem.at[1], {"gz": plane}).start()

    drains.append((zrecv.at[pl.ds(0, 2)], xs_sem.at[1]))

    loads[7].wait()
    rows = acc.shape[0]
    n_c = 4
    chunk = rows // n_c

    def full(a):
        return xz[:, a].reshape(n_g * xz.shape[2], width)

    arrived(zrecv.at[0], xr_sem.at[0])
    x2 = full(2)
    for c in range(n_c):
        span = pl.ds(c * chunk, chunk)
        acc[span, :] = sub_v[span, :].astype(F32) - nt(up2_v[span, :], x2)
    x_out[:, 2 * width :] = flipped(x2)
    loads[8].wait()
    for size, sem in early:
        sent(size, sem)
    fewer_if_own(sent, l_in, ls_sem)
    fewer_if_own(sent, csend, cs_sem)

    @pl.when(own)
    def _():
        for k in range(levels):
            sent(crecv, ys_sem.at[k])
        sent(frecv, vs_sem)

    arrived(zrecv.at[pl.ds(0, 2)], xr_sem.at[1])
    for a in range(2):
        x_out[:, a * width : (a + 1) * width] = full(a)
    for size, sem in drains[len(early) :]:
        sent(size, sem)


def store_kernel(xt_v, acc, up01_v, x_hbm, res_hbm, x_v, res_v, sem):
    width = x_v.shape[1]
    n_c = 4
    chunk = acc.shape[0] // n_c
    for a in range(2):
        x_v[a] = jnp.transpose(xt_v[:, a * width : (a + 1) * width].astype(F32)).astype(BF16)
    x_v[2] = xt_v[:, 2 * width :]
    copies = [pltpu.make_async_copy(x_v, x_hbm, sem.at[n_c])]
    x01 = x_v[0:2].reshape(2 * width, width)
    for c in range(n_c):
        span = pl.ds(c * chunk, chunk)
        term = jnp.dot(up01_v[span, :], x01, preferred_element_type=F32)
        res_v[span, :] = (acc[span, :] - term).astype(BF16)
        copies.append(pltpu.make_async_copy(res_v.at[span], res_hbm.at[span], sem.at[c]))
        copies[-1].start()
    copies[0].start()
    for c in copies:
        c.wait()


def per_device(dims, sep_rhs, diag_inverse, off_blocks, pattern, sub_solution, couple_low, couple_up):
    n_g, n_p, n_q, levels, width, n_b = dims
    sub = sub_solution.reshape(sub_solution.shape[-2:])
    low = couple_low.reshape(couple_low.shape[-2:])
    up = couple_up.reshape(couple_up.shape[-2:])
    rhs = sep_rhs.reshape(sep_rhs.shape[1:])
    inv = diag_inverse.reshape(diag_inverse.shape[1:])
    blk = off_blocks.reshape(levels, n_b, width, width)
    rows, cols = sub.shape
    piece = cols // n_g
    nb = n_p // n_q
    dma = pltpu.SemaphoreType.DMA
    wc = nb * width // n_g
    vmem = pltpu.VMEM
    xt, acc, up01 = pl.pallas_call(
        functools.partial(kernel, dims),
        out_shape=(vmem((cols, levels * width), BF16), vmem(sub.shape, F32), vmem((rows, 2 * width), BF16)),
        in_specs=[pl.BlockSpec(memory_space=pl.ANY)] * 7,
        out_specs=(pl.BlockSpec(memory_space=vmem),) * 3,
        scratch_shapes=[
            vmem(sub.shape, BF16),
            vmem(low.shape, BF16),
            vmem((rows, width), BF16),
            vmem(inv.shape, BF16),
            vmem(rhs.shape, BF16),
            vmem(blk.shape, BF16),
            pltpu.SMEM(pattern.shape, jnp.int32),
            vmem((levels * (levels - 1), width, nb * width), BF16),
            vmem((nb * width, 2 * width), BF16),
            vmem((nb * width, 2 * width), BF16),
            vmem((width, width), BF16),
            vmem((levels, n_g, piece, width), F32),
            vmem((levels, n_g, piece, width), BF16),
            vmem((levels, n_g - 1, piece, width), BF16),
            vmem((piece, width), BF16),
            vmem((n_q - 1, piece, width), BF16),
            vmem((3, piece, 2 * width), BF16),
            vmem((3, n_q - 1, piece, 2 * width), BF16),
            vmem((levels, piece, width), BF16),
            vmem((levels, nb, piece, width), BF16),
            vmem((nb, piece, width), BF16),
            vmem((n_p - 1, piece, width), BF16),
            vmem((nb, width, width), BF16),
            vmem((nb, width, width), BF16),
            vmem((n_g, levels, piece, width), BF16),
            vmem((width // wc, wc, width), BF16),
            vmem((n_p, wc, width), BF16),
            vmem((n_q - 1, width, nb * width), BF16),
            vmem((n_g, wc, width), BF16),
            dma((9,)),
            dma((2,)),
            dma((2,)),
            dma(()),
            dma(()),
            dma((3,)),
            dma((3,)),
            dma(()),
            dma(()),
            dma(()),
            dma(()),
            dma(()),
            dma(()),
            dma((levels,)),
            dma((levels,)),
            dma((2,)),
            dma((2,)),
            dma(()),
            dma(()),
            dma(()),
            dma(()),
            dma(()),
            dma(()),
        ],
        compiler_params=pltpu.CompilerParams(collective_id=0, has_side_effects=True),
    )(rhs, inv, blk, pattern, sub, low, up)
    x, res = pl.pallas_call(
        store_kernel,
        out_shape=(jax.ShapeDtypeStruct(rhs.shape, BF16), jax.ShapeDtypeStruct(sub.shape, BF16)),
        in_specs=[pl.BlockSpec(memory_space=vmem)] * 3,
        out_specs=(pl.BlockSpec(memory_space=pl.ANY),) * 2,
        scratch_shapes=[vmem(rhs.shape, BF16), vmem(sub.shape, BF16), dma((5,))],
    )(*(pltpu.with_memory_space_constraint(v, vmem) for v in (xt, acc, up01)))
    return x[None], res[None, None, None]


def solution(mesh):
    n_g, n_p, n_q = mesh.shape["gz"], mesh.shape["pr"], mesh.shape["pc"]

    def step(*args):
        levels, width = args[1].shape[1], args[1].shape[2]
        dims = (n_g, n_p, n_q, levels, width, args[2].shape[2])
        return per_device(dims, *args)

    return jax.shard_map(
        step,
        mesh=mesh,
        in_specs=(
            P("pr", None, None, None),
            P("pr", None, None, None),
            P("pr", None, None, "pc", None, None),
            P(),
            P("gz", "pr", "pc", None, None),
            P("gz", "pr", "pc", None, None),
            P("gz", "pr", "pc", None, None),
        ),
        out_specs=(P("pr", None, None, None), P("gz", "pr", "pc", None, None)),
        check_vma=False,
    )
```

```python
import functools

import jax
import jax.numpy as jnp
from jax import lax
from jax.experimental import pallas as pl
from jax.experimental.pallas import tpu as pltpu
from jax.sharding import PartitionSpec as P

F32 = jnp.float32
BF16 = jnp.bfloat16
MESH = pl.DeviceIdType.MESH


def nt(a, b):
    return lax.dot_general(a, b, (((1,), (1,)), ((), ())), preferred_element_type=F32)


def ring_order(n):
    return sorted(range(1, n), key=lambda r: (-min(r, n - r), r))


def kernel(
    dims,
    rhs_hbm, inv_hbm, blk_hbm, pat_hbm, sub_hbm, low_hbm, up_hbm,
    x_out, acc, up01_v,
    sub_v, low_v, up2_v, inv_v, rhs_v, blk_v, pat_s,
    w_v, wl_v, wu_v, inv_t, rhs_t, zsend, zrecv, fsend, frecv, esend, erecv, ysend, yrecv, csend, crecv, l_out, l_in, xz, u_piece, u_all, f_all, prod,
    in_sem, zs_sem, zr_sem, fs_sem, fr_sem, es_sem, er_sem, cs_sem, cr_sem, ls_sem, lr_sem, vs_sem, vr_sem, ys_sem, yr_sem, xs_sem, xr_sem, us_sem, ur_sem, ws_sem, wr_sem, ds_sem, dr_sem,
):
    n_g, n_p, n_q, levels, width, n_b = dims
    g = lax.axis_index("gz")
    p = lax.axis_index("pr")
    q = lax.axis_index("pc")
    nb = n_p // n_q
    own = lax.rem(p, n_q) == q
    own_b = p // n_q

    part_rows = prod.shape[1]
    halves = width // part_rows

    def z_peer(r):
        return {"gz": lax.rem(g + r, n_g)}

    def x_peer(r):
        return {"pc": lax.rem(q + r, n_q)}

    def y_peer(r):
        return {"pr": lax.rem(p + r, n_p)}

    def cross_peer(b):
        return {"pr": b * n_q + q, "pc": lax.rem(p, n_q)}

    barrier = pltpu.get_barrier_semaphore()
    @pl.when(jnp.logical_not(own))
    def _():
        for b in range(nb):
            pl.semaphore_signal(barrier, inc=1, device_id=cross_peer(b), device_id_type=MESH)

    for r in ring_order(n_g):
        pl.semaphore_signal(barrier, inc=1, device_id=z_peer(r), device_id_type=MESH)
    for r in ring_order(n_p):
        pl.semaphore_signal(barrier, inc=1, device_id=y_peer(r), device_id_type=MESH)
    for r in ring_order(n_q):
        pl.semaphore_signal(barrier, inc=1, device_id=x_peer(r), device_id_type=MESH)

    rest = pl.ds(width, (levels - 1) * width)
    pairs = (
        (sub_hbm, sub_v),
        (low_hbm.at[pl.ds(0, width)], low_v.at[pl.ds(0, width)]),
        (low_hbm.at[rest], low_v.at[rest]),
        (blk_hbm, blk_v),
        (pat_hbm, pat_s),
        (inv_hbm, inv_v),
        (rhs_hbm, rhs_v),
        (up_hbm.at[:, pl.ds(2 * width, width)], up2_v),
        (up_hbm.at[:, pl.ds(0, 2 * width)], up01_v),
    )
    loads = [pltpu.make_async_copy(a, b, in_sem.at[k]) for k, (a, b) in enumerate(pairs)]
    for c in loads:
        c.start()

    def remote(src, dst, ssem, rsem, peer):
        return pltpu.make_async_remote_copy(
            src_ref=src, dst_ref=dst, send_sem=ssem, recv_sem=rsem, device_id=peer, device_id_type=MESH
        )

    drains = []

    def send_all(copies, size, sem):
        for c in copies:
            c.start()
        drains.append((size, sem))

    def sent(size, sem):
        remote(size, size, sem, sem, x_peer(1)).wait_send()

    def arrived(size, sem):
        remote(size, size, sem, sem, x_peer(1)).wait_recv()

    def fewer_if_own(wait, ref, sem):
        @pl.when(own)
        def _():
            wait(ref.at[pl.ds(0, nb - 1)], sem)

        @pl.when(jnp.logical_not(own))
        def _():
            wait(ref, sem)


    def partial_update(a):
        part = jnp.dot(low_v[a * width : (a + 1) * width, :], sub_v[...], preferred_element_type=F32)
        turned = jnp.transpose(part).astype(BF16)
        zsend[a] = turned.reshape(n_g, turned.shape[0] // n_g, width)

    def z_copy(a, r):
        k = min(a, 1)
        return remote(zsend.at[a, lax.rem(g + r, n_g)], zrecv.at[a, r - 1], zs_sem, zr_sem.at[k], z_peer(r))

    others = pl.ds(1, levels - 1)

    loads[0].wait()
    loads[1].wait()
    partial_update(0)

    def slot_of(row_level, col_level):
        return row_level * (levels - 1) + (col_level if col_level < row_level else col_level - 1)

    def masked_blocks(row_level, col_level):
        for b in range(nb):
            i = row_level * n_p + p
            j = col_level * n_p + b * n_q + q
            mark = pat_s[i, j] if col_level < row_level else pat_s[j, i]
            block = blk_v[row_level, col_level * nb + b]
            w_v[slot_of(row_level, col_level), :, b * width : (b + 1) * width] = jnp.where(
                mark == 1, block, jnp.zeros_like(block)
            )

    def weights(row_level, col_level):
        return w_v[slot_of(row_level, col_level)]

    def folded(level, col_level):
        return jnp.dot(inv_v[level], weights(level, col_level), preferred_element_type=F32)

    def flipped(a):
        return jnp.transpose(a.astype(F32)).astype(BF16)

    for k in (3, 4, 5):
        loads[k].wait()
    masked_blocks(2, 1)
    step21 = folded(2, 1)
    for b in range(nb):
        l_out[b] = flipped(step21[:, b * width : (b + 1) * width])

    def l_copy(b):
        return remote(l_out.at[b], l_in.at[own_b], ls_sem, lr_sem, cross_peer(b))

    @pl.when(own)
    def _():
        l_in[own_b] = l_out[own_b]

    first, second = slot_of(0, 1), slot_of(1, 2)
    masked_blocks(0, 1)
    masked_blocks(1, 2)

    def f_copy(h, r):
        span = pl.ds(h * (nb * width // 2), nb * width // 2)
        return remote(w_v.at[first, :, span], f_all.at[r - 1, :, span], ws_sem, wr_sem, x_peer(r))

    def f_send(h):
        for r in ring_order(n_q):
            f_copy(h, r).start()

    def u_copy(r):
        return remote(u_piece.at[g % halves], u_all.at[p], us_sem, ur_sem, y_peer(r))

    def d_copy(r):
        return remote(prod.at[g], prod.at[g], ds_sem, dr_sem, z_peer(r))

    mine = w_v[second, :, pl.ds(pl.multiple_of(g // halves * width, width), width)]
    u_piece[...] = jnp.transpose(mine.astype(F32)).astype(BF16).reshape(halves, part_rows, width)
    u_all[p] = u_piece[g % halves]

    loads[2].wait()
    for a in range(1, levels):
        partial_update(a)
    pl.semaphore_wait(barrier, n_g + n_p + n_q - 3 + jnp.where(own, 0, nb))
    for r in ring_order(n_g):
        z_copy(0, r).start()
    f_send(0)
    for b in range(nb):

        @pl.when(b * n_q + q != p)
        def _(b=b):
            l_copy(b).start()

    send_all([u_copy(r) for r in ring_order(n_p)], u_all.at[pl.ds(0, n_p - 1)], us_sem)
    for a in range(1, levels):
        for r in ring_order(n_g):
            z_copy(a, r).start()
    drains.append((zrecv, zs_sem))

    for row_level in range(1, levels):
        masked_blocks(row_level, 0)
        wl_v[:, (row_level - 1) * width : row_level * width] = flipped(folded(row_level, 0))
    masked_blocks(0, 2)
    for k, w in enumerate((weights(0, 2), weights(1, 2))):
        wu_v[:, k * width : (k + 1) * width] = flipped(w)
    inv_t[...] = flipped(inv_v[0])
    loads[6].wait()
    for a in range(levels):
        rhs_t[a] = jnp.transpose(rhs_v[a].astype(F32)).reshape(n_g, rhs_t.shape[2], width)

    def form_product():
        arrived(u_all.at[pl.ds(0, n_p - 1)], ur_sem)
        arrived(f_all, wr_sem)
        total = None
        for r in range(n_q):
            left = weights(0, 1) if r == 0 else f_all[r - 1]
            from_q = lax.rem(q + n_q - r, n_q)
            right = jnp.concatenate([u_all[b * n_q + from_q] for b in range(nb)], axis=1)
            term = nt(right, left)
            total = term if total is None else total + term
        prod[g] = total.astype(BF16)
        send_all([d_copy(r) for r in ring_order(n_g)], prod.at[pl.ds(0, n_g - 1)], ds_sem)

    def product():
        arrived(prod.at[pl.ds(0, n_g - 1)], dr_sem)
        return prod[...].reshape(n_g * part_rows, width)

    def z_total(a):
        total = zsend[a, g].astype(F32)
        for r in range(1, n_g):
            total = total + zrecv[a, r - 1].astype(F32)
        return total.astype(BF16)

    def exchange(value, src, dst, ssem, rsem):
        src[...] = value
        for r in ring_order(n_q):
            remote(src, dst.at[r - 1], ssem, rsem, x_peer(r)).start()

    def collected(value, dst, rsem):
        arrived(dst, rsem)
        half = n_q // 2
        total = None
        for k in range(half):
            start = value.astype(F32) if k == 0 else dst[k - 1].astype(F32)
            pair = start + dst[k + half - 1].astype(F32)
            total = pair if total is None else total + pair
        return total

    def y_copy(k, r):
        return remote(ysend.at[k], yrecv.at[k, own_b], ys_sem.at[k], yr_sem.at[k], y_peer(r))

    def broadcast_own(k, value):
        ysend[k] = value
        for r in ring_order(n_p):
            y_copy(k, r).start()
        yrecv[k, own_b] = value

    def gathered(k):
        fewer_if_own(arrived, yrecv.at[k], yr_sem.at[k])
        return jnp.concatenate([yrecv[k, b] for b in range(nb)], axis=1)

    def solve(a, resid):
        return nt(resid.astype(BF16), inv_v[a])

    arrived(zrecv.at[0], zr_sem.at[0])
    value = z_total(0)
    exchange(value, fsend, frecv, fs_sem, fr_sem)
    resid = (rhs_t[0, g] - collected(value, frecv, fr_sem)).astype(BF16)
    y0 = jnp.dot(resid, inv_t[...], preferred_element_type=F32).astype(BF16)

    @pl.when(own)
    def _():
        broadcast_own(0, y0)

    arrived(zrecv.at[others], zr_sem.at[1])
    both = jnp.concatenate([z_total(a) for a in (1, 2)], axis=1)
    exchange(both, esend.at[0], erecv.at[0], es_sem, er_sem.at[0])
    total = collected(both, erecv.at[0], er_sem.at[0])
    solved1 = solve(1, rhs_t[1, g] - total[:, :width])
    solved2 = solve(2, rhs_t[2, g] - total[:, width:])

    both = jnp.dot(gathered(0), wl_v[...], preferred_element_type=F32).astype(BF16)
    exchange(both, esend.at[1], erecv.at[1], es_sem, er_sem.at[1])
    f_send(1)
    drains.append((f_all, ws_sem))
    fewer_if_own(arrived, l_in, lr_sem)
    step2 = jnp.concatenate([l_in[b] for b in range(nb)], axis=1)
    total = collected(both, erecv.at[1], er_sem.at[1])
    y1 = (solved1 - total[:, :width]).astype(BF16)
    rest2 = solved2 - total[:, width:]
    terms = jnp.dot(y1, step2, preferred_element_type=F32).astype(BF16)
    for b in range(nb):
        csend[b] = terms[:, b * width : (b + 1) * width]
    for b in range(nb):

        @pl.when(b * n_q + q != p)
        def _(b=b):
            ahead = lax.rem(b * n_q + q + n_p - p, n_p) - 1
            remote(csend.at[b], crecv.at[ahead], cs_sem, cr_sem, {"pr": b * n_q + q}).start()

    @pl.when(own)
    def _():
        broadcast_own(1, y1)

    form_product()

    @pl.when(own)
    def _():
        arrived(crecv, cr_sem)
        sum2 = csend[own_b].astype(F32)
        for r in range(1, n_p):
            sum2 = sum2 + crecv[r - 1].astype(F32)
        y2 = (rest2 - sum2).astype(BF16)
        broadcast_own(2, y2)
        mine = xz.at[g, levels - 1]
        mine[...] = y2
        for r in ring_order(n_q):
            remote(mine, mine, vs_sem, vr_sem, x_peer(r)).start()

    drains.append((frecv, fs_sem))
    drains.append((erecv, es_sem))

    part0 = nt(gathered(1), weights(0, 1))
    weights0 = product()
    wu_v[:, :width] = (wu_v[:, :width].astype(F32) - weights0.astype(F32)).astype(BF16)
    both = jnp.dot(gathered(2), wu_v[...], preferred_element_type=F32)
    both = jnp.concatenate([both[:, :width] + part0, both[:, width:]], axis=1).astype(BF16)
    exchange(both, esend.at[2], erecv.at[2], es_sem, er_sem.at[2])

    @pl.when(jnp.logical_not(own))
    def _():
        arrived(xz.at[g, levels - 1], vr_sem)

    last = xz.at[g, pl.ds(levels - 1, 1)]
    copies = [remote(last, last, xs_sem, xr_sem.at[0], z_peer(r)) for r in ring_order(n_g)]
    for c in copies:
        c.start()
    total = collected(both, erecv.at[2], er_sem.at[2])
    xz[g, 0] = (y0.astype(F32) - total[:, :width]).astype(BF16)
    xz[g, 1] = (y1.astype(F32) - total[:, width:]).astype(BF16)
    early = list(drains)
    mine = xz.at[g, pl.ds(0, 2)]
    for plane in range(n_g):

        @pl.when(g != plane)
        def _(plane=plane):
            remote(mine, mine, xs_sem, xr_sem.at[1], {"gz": plane}).start()

    drains.append((zrecv, xs_sem))

    loads[7].wait()
    rows = acc.shape[0]
    n_c = 4
    chunk = rows // n_c

    def full(a):
        return xz[:, a].reshape(n_g * xz.shape[2], width)

    arrived(zrecv.at[0], xr_sem.at[0])
    x2 = full(2)
    for c in range(n_c):
        span = pl.ds(c * chunk, chunk)
        acc[span, :] = sub_v[span, :].astype(F32) - nt(up2_v[span, :], x2)
    x_out[:, 2 * width :] = flipped(x2)
    loads[8].wait()
    for size, sem in early:
        sent(size, sem)
    fewer_if_own(sent, l_in, ls_sem)
    fewer_if_own(sent, csend, cs_sem)

    @pl.when(own)
    def _():
        for k in range(levels):
            sent(crecv, ys_sem.at[k])
        sent(frecv, vs_sem)

    arrived(zrecv.at[pl.ds(0, 2)], xr_sem.at[1])
    for a in range(2):
        x_out[:, a * width : (a + 1) * width] = full(a)
    for size, sem in drains[len(early) :]:
        sent(size, sem)


def store_kernel(xt_v, acc, up01_v, x_hbm, res_hbm, x_v, res_v, sem):
    width = x_v.shape[1]
    n_c = 4
    chunk = acc.shape[0] // n_c
    for a in range(2):
        x_v[a] = jnp.transpose(xt_v[:, a * width : (a + 1) * width].astype(F32)).astype(BF16)
    x_v[2] = xt_v[:, 2 * width :]
    copies = [pltpu.make_async_copy(x_v, x_hbm, sem.at[n_c])]
    x01 = x_v[0:2].reshape(2 * width, width)
    for c in range(n_c):
        span = pl.ds(c * chunk, chunk)
        term = jnp.dot(up01_v[span, :], x01, preferred_element_type=F32)
        res_v[span, :] = (acc[span, :] - term).astype(BF16)
        copies.append(pltpu.make_async_copy(res_v.at[span], res_hbm.at[span], sem.at[c]))
        copies[-1].start()
    copies[0].start()
    for c in copies:
        c.wait()


def per_device(dims, sep_rhs, diag_inverse, off_blocks, pattern, sub_solution, couple_low, couple_up):
    n_g, n_p, n_q, levels, width, n_b = dims
    sub = sub_solution.reshape(sub_solution.shape[-2:])
    low = couple_low.reshape(couple_low.shape[-2:])
    up = couple_up.reshape(couple_up.shape[-2:])
    rhs = sep_rhs.reshape(sep_rhs.shape[1:])
    inv = diag_inverse.reshape(diag_inverse.shape[1:])
    blk = off_blocks.reshape(levels, n_b, width, width)
    rows, cols = sub.shape
    piece = cols // n_g
    nb = n_p // n_q
    dma = pltpu.SemaphoreType.DMA
    wc = nb * width // n_g
    vmem = pltpu.VMEM
    xt, acc, up01 = pl.pallas_call(
        functools.partial(kernel, dims),
        out_shape=(vmem((cols, levels * width), BF16), vmem(sub.shape, F32), vmem((rows, 2 * width), BF16)),
        in_specs=[pl.BlockSpec(memory_space=pl.ANY)] * 7,
        out_specs=(pl.BlockSpec(memory_space=vmem),) * 3,
        scratch_shapes=[
            vmem(sub.shape, BF16),
            vmem(low.shape, BF16),
            vmem((rows, width), BF16),
            vmem(inv.shape, BF16),
            vmem(rhs.shape, BF16),
            vmem(blk.shape, BF16),
            pltpu.SMEM(pattern.shape, jnp.int32),
            vmem((levels * (levels - 1), width, nb * width), BF16),
            vmem((nb * width, 2 * width), BF16),
            vmem((nb * width, 2 * width), BF16),
            vmem((width, width), BF16),
            vmem((levels, n_g, piece, width), F32),
            vmem((levels, n_g, piece, width), BF16),
            vmem((levels, n_g - 1, piece, width), BF16),
            vmem((piece, width), BF16),
            vmem((n_q - 1, piece, width), BF16),
            vmem((3, piece, 2 * width), BF16),
            vmem((3, n_q - 1, piece, 2 * width), BF16),
            vmem((levels, piece, width), BF16),
            vmem((levels, nb, piece, width), BF16),
            vmem((nb, piece, width), BF16),
            vmem((n_p - 1, piece, width), BF16),
            vmem((nb, width, width), BF16),
            vmem((nb, width, width), BF16),
            vmem((n_g, levels, piece, width), BF16),
            vmem((width // wc, wc, width), BF16),
            vmem((n_p, wc, width), BF16),
            vmem((n_q - 1, width, nb * width), BF16),
            vmem((n_g, wc, width), BF16),
            dma((9,)),
            dma(()),
            dma((2,)),
            dma(()),
            dma(()),
            dma(()),
            dma((3,)),
            dma(()),
            dma(()),
            dma(()),
            dma(()),
            dma(()),
            dma(()),
            dma((levels,)),
            dma((levels,)),
            dma(()),
            dma((2,)),
            dma(()),
            dma(()),
            dma(()),
            dma(()),
            dma(()),
            dma(()),
        ],
        compiler_params=pltpu.CompilerParams(collective_id=0, has_side_effects=True),
    )(rhs, inv, blk, pattern, sub, low, up)
    x, res = pl.pallas_call(
        store_kernel,
        out_shape=(jax.ShapeDtypeStruct(rhs.shape, BF16), jax.ShapeDtypeStruct(sub.shape, BF16)),
        in_specs=[pl.BlockSpec(memory_space=vmem)] * 3,
        out_specs=(pl.BlockSpec(memory_space=pl.ANY),) * 2,
        scratch_shapes=[vmem(rhs.shape, BF16), vmem(sub.shape, BF16), dma((5,))],
    )(*(pltpu.with_memory_space_constraint(v, vmem) for v in (xt, acc, up01)))
    return x[None], res[None, None, None]


def solution(mesh):
    n_g, n_p, n_q = mesh.shape["gz"], mesh.shape["pr"], mesh.shape["pc"]

    def step(*args):
        levels, width = args[1].shape[1], args[1].shape[2]
        dims = (n_g, n_p, n_q, levels, width, args[2].shape[2])
        return per_device(dims, *args)

    return jax.shard_map(
        step,
        mesh=mesh,
        in_specs=(
            P("pr", None, None, None),
            P("pr", None, None, None),
            P("pr", None, None, "pc", None, None),
            P(),
            P("gz", "pr", "pc", None, None),
            P("gz", "pr", "pc", None, None),
            P("gz", "pr", "pc", None, None),
        ),
        out_specs=(P("pr", None, None, None), P("gz", "pr", "pc", None, None)),
        check_vma=False,
    )
```
